512 devices in a mesh: group: 16 (over x_lo, z), space: 32 (over x_hi, y, core).
Axes of the slice: x: 4 (x_hi: 2, x_lo: 2; x = x_hi * 2 + x_lo), y: 8, z: 8, core: 2. Of those that a mesh axis runs over, the one named last changes fastest.
Arguments:
- pressure: float32 [1024, 512, 128], P('space', 'group'), may hold values from -6 to 6
- source: float32 [1024, 512, 128], P('space', 'group'), may hold values from -4 to 4
- labels: int32 [1024, 512], P('space', 'group'), may hold values from 0 to 15
- region_table: float32 [16, 128], replicated, may hold values from 0.05 to 2
Outputs:
- residual: float32 [1024, 512, 128], P('space', 'group')
- correction: float32 [1024, 512, 128], P('space', 'group')
The draws below stay inside these ranges and needn't reach their ends.
All inputs are finite; a program needn't handle non-finite values.
Results may differ from the reference program's by a relative error of at most 0.00013.
Values sent between devices are 32-bit elements; how exact they have to be, the bound alone decides.
A program may use at most 64 MiB of HBM per device.

```python
import math
import jax
import jax.numpy as jnp
from jax import lax

NZ = 128
REGIONS = 16
SWEEPS = 4
FACTOR = 4
NX = 1024
NY = 512
NXC = 256
NYC = 128


def draw_source(key, part):
    rough = jax.random.normal(key, (NX, NY, NZ), jnp.float32)
    return jnp.clip(rough, -4.0, 4.0)


def plant(values, rng, smallest, largest):
    longest = values.shape.index(max(values.shape))
    spots = []
    for shift in (0, 1):
        where = [jax.random.randint(jax.random.fold_in(rng, axis), (), 0, length) for axis, length in enumerate(values.shape)]
        where[longest] = (where[longest] + shift) % values.shape[longest]
        spots.append(tuple(where))
    return values.at[spots[0]].set(smallest).at[spots[1]].set(largest)


def steps_of(key, shape, cuts, low, top_value):
    def one(position, blocks):
        draws = jax.random.uniform(jax.random.fold_in(jax.random.fold_in(key, 6), position), (blocks,), jnp.float32, low / len(cuts), top_value / len(cuts))
        return jnp.repeat(jnp.exp(draws), shape[position] // blocks).reshape((-1,) + (1,) * (len(shape) - position - 1))

    level = one(*cuts[0])
    for cut in cuts[1:]:
        level = level * one(*cut)
    return level


def normal_values(own_key, shape, scale, limit, pieces=(), held_as=jnp.bfloat16):
    result = scale * jax.random.normal(own_key, shape, jnp.float32)
    if pieces:
        result = result * steps_of(own_key, shape, pieces, -0.22, 0.18)
    return jnp.clip(result, -limit, limit).astype(held_as)


def setup_inputs(seed: int = 0) -> dict:
    keys = jax.random.split(jax.random.key(seed), 5)
    return {
        "pressure": normal_values(keys[0], (NX, NY, NZ), 1.0, 6.0, ((0, 32), (1, 16)), jnp.float32),
        "source": draw_source(jax.random.fold_in(keys[4], 71), 0),
        "labels": plant(jax.random.randint(keys[2], (NX, NY), 0, REGIONS), jax.random.fold_in(keys[2], 1), 0, REGIONS - 1).astype(jnp.int32),
        "region_table": jnp.clip(jnp.exp(jax.random.uniform(keys[3], (REGIONS, NZ), jnp.float32, math.log(0.05), math.log(2.0))), 0.05, 2.0),
    }


relax_weight = 0.8
centre_weight = 0.5
side_weight = 0.125


def face_weights(coeff_pad, scale):
    rows = coeff_pad.shape[0] - 2
    cols = coeff_pad.shape[1] - 2
    centre = coeff_pad[1:-1, 1:-1]
    depth = centre.shape[2]
    faces = []
    for shift_x, shift_y in ((2, 1), (0, 1), (1, 2), (1, 0)):
        nearby = coeff_pad[shift_x:shift_x + rows, shift_y:shift_y + cols]
        faces.append(scale * 0.5 * (centre + nearby))
    column = jnp.pad(centre, ((0, 0), (0, 0), (1, 1)))
    for shift_z in (2, 0):
        faces.append(0.5 * (centre + column[:, :, shift_z:shift_z + depth]))
    diagonal = faces[0]
    for face in faces[1:]:
        diagonal = diagonal + face
    return faces, diagonal


def apply_faces(field_pad, faces):
    rows = field_pad.shape[0] - 2
    cols = field_pad.shape[1] - 2
    centre = field_pad[1:-1, 1:-1]
    depth = centre.shape[2]
    column = jnp.pad(centre, ((0, 0), (0, 0), (1, 1)))
    nearby = [field_pad[sx:sx + rows, sy:sy + cols] for sx, sy in ((2, 1), (0, 1), (1, 2), (1, 0))]
    nearby = nearby + [column[:, :, sz:sz + depth] for sz in (2, 0)]
    total = faces[0] * (centre - nearby[0])
    for index in range(1, 6):
        total = total + faces[index] * (centre - nearby[index])
    return total


def blend(padded):
    centre = padded[1:-1, 1:-1]
    sides = padded[2:, 1:-1] + padded[:-2, 1:-1]
    sides = sides + padded[1:-1, 2:]
    sides = sides + padded[1:-1, :-2]
    return centre_weight * centre + side_weight * sides


def pad_plane(field):
    return jnp.pad(field, ((1, 1), (1, 1), (0, 0)))


def reference(pressure, source, labels, region_table):
    coeff = region_table[labels]
    faces, _ = face_weights(pad_plane(coeff), 1.0)
    residual = source - apply_faces(pad_plane(pressure), faces)
    restricted = blend(pad_plane(residual))
    scale = 1.0

    def regroup(field):
        return field.reshape(NXC, FACTOR, NYC, FACTOR, NZ).transpose(1, 3, 0, 2, 4).reshape(FACTOR * FACTOR, NXC, NYC, NZ)

    def smooth(pair):
        rhs, coarse_coeff = pair
        coarse_faces, diagonal = face_weights(pad_plane(coarse_coeff), scale)
        iterate = relax_weight * rhs / diagonal
        for sweep in range(SWEEPS - 1):
            iterate = iterate + relax_weight * (rhs - apply_faces(pad_plane(iterate), coarse_faces)) / diagonal
        return iterate

    coarse = lax.map(smooth, (regroup(restricted), regroup(coeff)))
    spread = coarse.reshape(FACTOR, FACTOR, NXC, NYC, NZ).transpose(2, 0, 3, 1, 4).reshape(NX, NY, NZ)
    correction = blend(pad_plane(spread))
    return residual, correction
```

```python
import jax
import jax.numpy as jnp
from jax import lax
from jax.experimental import pallas as pl
from jax.experimental.pallas import tpu as pltpu
from jax.sharding import PartitionSpec as P

MESH = pl.DeviceIdType.MESH
N = 32
DEPTH = 128
XO, YO = 17, 20
NXF, NYF = 66, 72
DIRS = [(dx, dy) for dx in (-1, 0, 1) for dy in (-1, 0, 1) if (dx, dy) != (0, 0)]
SIDES = [(-1, 0), (1, 0), (0, -1), (0, 1)]


def span(step, width, origin):
    if step == 1:
        return origin + N - width, origin - width
    if step == -1:
        return origin, origin + N
    return origin, origin


def kernel(p_hbm, src_hbm, lab_hbm, tab_hbm, res_hbm, cor_hbm,
           pb, sb, tb, lb, lt, rb, s_ref, w_ref, k_ref, ua, pa, ub, qb, uc, ob,
           send, recv, local):
    groups = lax.axis_size("group")
    spaces = lax.axis_size("space")
    gi = lax.axis_index("group")
    si = lax.axis_index("space")

    def there(d):
        dx, dy = d
        ok = None
        if dx == 1:
            ok = si < spaces - 1
        elif dx == -1:
            ok = si > 0
        if dy:
            okg = gi < groups - 1 if dy == 1 else gi > 0
            ok = okg if ok is None else jnp.logical_and(ok, okg)
        return ok

    def back(d):
        return (-d[0], -d[1])

    def device(d):
        return (gi + d[1], si + d[0])

    load_p = pltpu.make_async_copy(p_hbm, pb.at[pl.ds(1, N), pl.ds(4, N), :], local.at[0])
    load_s = pltpu.make_async_copy(src_hbm, sb, local.at[1])
    load_l = pltpu.make_async_copy(lab_hbm, lb.at[1, pl.ds(N, N), :], local.at[2])
    load_t = pltpu.make_async_copy(tab_hbm, tb, local.at[3])
    load_l.start()
    load_t.start()
    load_p.start()
    load_s.start()

    barrier = pltpu.get_barrier_semaphore()
    count = jnp.int32(0)
    for d in DIRS:
        ok = there(d)
        count = count + ok.astype(jnp.int32)

        @pl.when(ok)
        def _():
            pl.semaphore_signal(barrier, 1, device_id=device(d), device_id_type=MESH)

    for d in DIRS:
        @pl.when(jnp.logical_not(there(d)))
        def _():
            dx, dy = d
            lb[1 + dy, pl.ds(N * (1 + dx), N), :] = jnp.full((N, N), -1, jnp.int32)

    for d in SIDES:
        @pl.when(jnp.logical_not(there(d)))
        def _():
            dx, dy = d
            if dx:
                pb[0 if dx < 0 else N + 1] = jnp.zeros((40, DEPTH), jnp.float32)
                r0 = XO - 14 if dx < 0 else XO + N

                @pl.loop(0, 14)
                def _(i):
                    rb[r0 + i] = jnp.zeros((NYF, DEPTH), jnp.float32)
            else:
                col = 3 if dy < 0 else 4 + N
                pb[pl.ds(1, N), pl.ds(col, 1), :] = jnp.zeros((N, 1, DEPTH), jnp.float32)
                c0 = YO - 14 if dy < 0 else YO + N

                @pl.loop(XO - 14, XO + N + 14)
                def _(i):
                    rb[i, pl.ds(c0, 14), :] = jnp.zeros((14, DEPTH), jnp.float32)

    pl.semaphore_wait(barrier, count)

    def message(kind, d):
        dx, dy = d
        if kind == 0:
            at = DIRS.index(d)
            src = lab_hbm
            dst = lb.at[1 - dy, pl.ds(N * (1 - dx), N), :]
        elif kind == 1:
            at = 8 + SIDES.index(d)
            if dx:
                src = p_hbm.at[pl.ds(N - 1 if dx > 0 else 0, 1)]
                dst = pb.at[pl.ds(0 if dx > 0 else N + 1, 1), pl.ds(4, N), :]
            else:
                src = p_hbm.at[:, pl.ds(N - 1 if dy > 0 else 0, 1), :]
                dst = pb.at[pl.ds(1, N), pl.ds(3 if dy > 0 else 4 + N, 1), :]
        else:
            at = 12 + DIRS.index(d)
            wide = 14 if dx == 0 or dy == 0 else 13
            sx, tx = span(dx, wide, XO)
            sy, ty = span(dy, wide, YO)
            nx = wide if dx else N
            ny = wide if dy else N
            src = rb.at[pl.ds(sx, nx), pl.ds(sy, ny), :]
            dst = rb.at[pl.ds(tx, nx), pl.ds(ty, ny), :]
        return pltpu.make_async_remote_copy(
            src_ref=src, dst_ref=dst, send_sem=send.at[at], recv_sem=recv.at[at],
            device_id=device(d), device_id_type=MESH)

    def start(kind, dirs):
        for d in dirs:
            @pl.when(there(d))
            def _():
                message(kind, d).start()

    def arrive(kind, dirs):
        for d in dirs:
            @pl.when(there(back(d)))
            def _():
                message(kind, d).wait_recv()

    def sent(kind, dirs):
        for d in dirs:
            @pl.when(there(d))
            def _():
                message(kind, d).wait_send()

    start(1, SIDES)
    start(0, DIRS)

    load_t.wait()
    half = 0.5 * tb[...]
    lane = lax.broadcasted_iota(jnp.int32, (16, DEPTH), 1)
    up = jnp.where(lane < DEPTH - 1, pltpu.roll(half, DEPTH - 1, 1), 0.0)
    down = jnp.where(lane > 0, pltpu.roll(half, 1, 1), 0.0)
    wup = jnp.where(lane < DEPTH - 1, half + up, 0.0)
    vert = 6.0 * half + (up + down)
    wide = jnp.concatenate([half, wup, vert], axis=1)
    hi = wide.astype(jnp.bfloat16)
    rest = wide - hi.astype(jnp.float32)
    mid = rest.astype(jnp.bfloat16)
    low = (rest - mid.astype(jnp.float32)).astype(jnp.bfloat16)
    table = jnp.concatenate(
        [hi, mid, low, jnp.zeros((DEPTH - 48, 3 * DEPTH), jnp.bfloat16)], axis=0)

    load_l.wait()
    arrive(0, DIRS)
    t0 = lb[0].T
    t1 = lb[1].T
    t2 = lb[2].T
    pad = jnp.full((N, DEPTH - 96), -1, jnp.int32)
    lt[pl.ds(0, 20), :] = jnp.concatenate([t0, pad], axis=1)[12:]
    lt[pl.ds(20, N), :] = jnp.concatenate([t1, pad], axis=1)
    lt[pl.ds(52, 20), :] = jnp.concatenate([t2, pad], axis=1)[:20]

    lanes = lax.broadcasted_iota(jnp.int32, (NYF, DEPTH), 1)
    slot = jnp.where(lanes < 48, lanes & 15, -9)

    @pl.loop(0, NXF)
    def _(x):
        turned = pltpu.roll(lt[...], DEPTH - (x + N - XO), 1)
        tag = jnp.broadcast_to(turned[:, 0:1], (NYF, DEPTH))
        onehot = jnp.where(tag == slot, 1.0, 0.0).astype(jnp.bfloat16)
        out = jnp.dot(onehot, table, preferred_element_type=jnp.float32)
        s_ref[x] = out[:, :DEPTH]
        w_ref[x] = out[:, DEPTH:2 * DEPTH]
        k_ref[x] = out[:, 2 * DEPTH:]

    def vertical(weight, value):
        return weight * pltpu.roll(value, DEPTH - 1, 1) + pltpu.roll(weight * value, 1, 1)

    load_p.wait()
    load_s.wait()
    arrive(1, SIDES)

    @pl.loop(0, N)
    def _(x):
        fx = x + XO
        own = pl.ds(YO, N)
        s = s_ref[fx, own, :]
        sn = [s_ref[fx - 1, own, :], s_ref[fx + 1, own, :],
              s_ref[fx, pl.ds(YO - 1, N), :], s_ref[fx, pl.ds(YO + 1, N), :]]
        p = pb[x + 1, pl.ds(4, N), :]
        pn = [pb[x, pl.ds(4, N), :], pb[x + 2, pl.ds(4, N), :],
              pb[x + 1, pl.ds(3, N), :], pb[x + 1, pl.ds(5, N), :]]
        flow = (s + sn[0]) * (p - pn[0])
        for i in range(1, 4):
            flow = flow + (s + sn[i]) * (p - pn[i])
        both = k_ref[fx, own, :] - 4.0 * s
        flow = flow + (both * p - vertical(w_ref[fx, own, :], p))
        rb[fx, own, :] = sb[x] - flow

    start(2, DIRS)
    out_r = pltpu.make_async_copy(rb.at[pl.ds(XO, N), pl.ds(YO, N), :], res_hbm, local.at[4])
    out_r.start()

    @pl.loop(4, NXF - 4)
    def _(x):
        at = pl.ds(4, 64)
        s = s_ref[x, at, :]
        diag = (k_ref[x, at, :] + (s_ref[x - 4, at, :] + s_ref[x + 4, at, :])
                + (s_ref[x, pl.ds(0, 64), :] + s_ref[x, pl.ds(8, 64), :]))
        k_ref[x, at, :] = jnp.where(s > 0.0, 0.8 / diag, 0.0)

    arrive(2, DIRS)

    @pl.loop(4, NXF - 4)
    def _(x):
        at = pl.ds(4, 64)
        mean = (0.5 * rb[x, at, :]
                + 0.125 * (rb[x - 1, at, :] + rb[x + 1, at, :]
                           + rb[x, pl.ds(3, 64), :] + rb[x, pl.ds(5, 64), :]))
        u = k_ref[x, at, :] * mean
        sb2 = s_ref[x, at, :]
        ua[x, at, :] = u
        pa[x, at, :] = sb2 * u

    def sweep(first, u_in, p_in, u_out, p_out, base):
        y0, ny = first, NYF - 2 * first

        @pl.loop(first, NXF - first)
        def _(x):
            at = pl.ds(y0, ny)
            lo = pl.ds(y0 - 4, ny)
            hi_ = pl.ds(y0 + 4, ny)
            s = s_ref[x, at, :]
            u = u_in[x, at, :]
            un = (u_in[x - 4, at, :] + u_in[x + 4, at, :]
                  + u_in[x, lo, :] + u_in[x, hi_, :])
            pn = (p_in[x - 4, at, :] + p_in[x + 4, at, :]
                  + p_in[x, lo, :] + p_in[x, hi_, :])
            total = s * un + pn + vertical(w_ref[x, at, :], u)
            new = base[x, at, :] + 0.2 * u + k_ref[x, at, :] * total
            u_out[x, at, :] = new
            if p_out is not None:
                p_out[x, at, :] = s * new

    sweep(8, ua, pa, ub, qb, ua)
    sweep(12, ub, qb, uc, pa, ua)
    sweep(16, uc, pa, ub, None, ua)

    @pl.loop(0, N)
    def _(x):
        fx = x + XO
        at = pl.ds(YO, N)
        ob[x] = (0.5 * ub[fx, at, :]
                 + 0.125 * (ub[fx - 1, at, :] + ub[fx + 1, at, :]
                            + ub[fx, pl.ds(YO - 1, N), :] + ub[fx, pl.ds(YO + 1, N), :]))

    out_c = pltpu.make_async_copy(ob, cor_hbm, local.at[5])
    out_c.start()
    sent(0, DIRS)
    sent(1, SIDES)
    sent(2, DIRS)
    out_r.wait()
    out_c.wait()


def per_device(pressure, source, labels, region_table):
    any_ = pl.BlockSpec(memory_space=pl.ANY)
    own = jax.ShapeDtypeStruct((N, N, DEPTH), jnp.float32)
    field = pltpu.VMEM((NXF, NYF, DEPTH), jnp.float32)
    return pl.pallas_call(
        kernel,
        out_shape=(own, own),
        in_specs=[any_] * 4,
        out_specs=(any_, any_),
        scratch_shapes=[
            pltpu.VMEM((N + 2, 40, DEPTH), jnp.float32),
            pltpu.VMEM((N, N, DEPTH), jnp.float32),
            pltpu.VMEM((16, DEPTH), jnp.float32),
            pltpu.VMEM((3, 3 * N, N), jnp.int32),
            pltpu.VMEM((NYF, DEPTH), jnp.int32),
            field, field, field, field, field, field, field, field, field,
            pltpu.VMEM((N, N, DEPTH), jnp.float32),
            pltpu.SemaphoreType.DMA((20,)),
            pltpu.SemaphoreType.DMA((20,)),
            pltpu.SemaphoreType.DMA((6,)),
        ],
        compiler_params=pltpu.CompilerParams(collective_id=0, has_side_effects=True),
        name="correction",
    )(pressure, source, labels, region_table)


def solution(mesh):
    placed = (P("space", "group", None), P("space", "group", None), P("space", "group"), P())
    return jax.shard_map(
        per_device,
        mesh=mesh,
        in_specs=placed,
        out_specs=(P("space", "group", None), P("space", "group", None)),
        check_vma=False,
    )
```

```python
import jax
import jax.numpy as jnp
from jax import lax
from jax.experimental import pallas as pl
from jax.experimental.pallas import tpu as pltpu
from jax.sharding import PartitionSpec as P

MESH = pl.DeviceIdType.MESH
N = 32
DEPTH = 128
XO, YO = 17, 20
NXF, NYF = 66, 72
DIRS = [(dx, dy) for dx in (-1, 0, 1) for dy in (-1, 0, 1) if (dx, dy) != (0, 0)]
SIDES = [(-1, 0), (1, 0), (0, -1), (0, 1)]


def span(step, width, origin):
    if step == 1:
        return origin + N - width, origin - width
    if step == -1:
        return origin, origin + N
    return origin, origin


def exchange(p_hbm, src_hbm, lab_hbm, tab_hbm, s_ref, w_ref, k_ref, rb,
             pb, sb, tb, lb, lt, send, recv, local):
    groups = lax.axis_size("group")
    spaces = lax.axis_size("space")
    gi = lax.axis_index("group")
    si = lax.axis_index("space")

    def there(d):
        dx, dy = d
        ok = None
        if dx == 1:
            ok = si < spaces - 1
        elif dx == -1:
            ok = si > 0
        if dy:
            okg = gi < groups - 1 if dy == 1 else gi > 0
            ok = okg if ok is None else jnp.logical_and(ok, okg)
        return ok

    def back(d):
        return (-d[0], -d[1])

    def device(d):
        return (gi + d[1], si + d[0])

    load_p = pltpu.make_async_copy(p_hbm, pb.at[pl.ds(1, N), pl.ds(4, N), :], local.at[0])
    load_s = pltpu.make_async_copy(src_hbm, sb, local.at[1])
    load_l = pltpu.make_async_copy(lab_hbm, lb.at[1, pl.ds(N, N), :], local.at[2])
    load_t = pltpu.make_async_copy(tab_hbm, tb, local.at[3])
    load_l.start()
    load_t.start()
    load_p.start()
    load_s.start()

    barrier = pltpu.get_barrier_semaphore()
    count = jnp.int32(0)
    for d in DIRS:
        ok = there(d)
        count = count + ok.astype(jnp.int32)

        @pl.when(ok)
        def _():
            pl.semaphore_signal(barrier, 1, device_id=device(d), device_id_type=MESH)

    for d in DIRS:
        @pl.when(jnp.logical_not(there(d)))
        def _():
            dx, dy = d
            lb[1 + dy, pl.ds(N * (1 + dx), N), :] = jnp.full((N, N), -1, jnp.int32)

    for d in SIDES:
        @pl.when(jnp.logical_not(there(d)))
        def _():
            dx, dy = d
            if dx:
                pb[0 if dx < 0 else N + 1] = jnp.zeros((40, DEPTH), jnp.float32)
                r0 = XO - 14 if dx < 0 else XO + N

                @pl.loop(0, 14)
                def _(i):
                    rb[r0 + i] = jnp.zeros((NYF, DEPTH), jnp.float32)
            else:
                col = 3 if dy < 0 else 4 + N
                pb[pl.ds(1, N), pl.ds(col, 1), :] = jnp.zeros((N, 1, DEPTH), jnp.float32)
                c0 = YO - 14 if dy < 0 else YO + N

                @pl.loop(XO - 14, XO + N + 14)
                def _(i):
                    rb[i, pl.ds(c0, 14), :] = jnp.zeros((14, DEPTH), jnp.float32)

    pl.semaphore_wait(barrier, count)

    def message(kind, d):
        dx, dy = d
        if kind == 0:
            at = DIRS.index(d)
            src = lab_hbm
            dst = lb.at[1 - dy, pl.ds(N * (1 - dx), N), :]
        elif kind == 1:
            at = 8 + SIDES.index(d)
            if dx:
                src = p_hbm.at[pl.ds(N - 1 if dx > 0 else 0, 1)]
                dst = pb.at[pl.ds(0 if dx > 0 else N + 1, 1), pl.ds(4, N), :]
            else:
                src = p_hbm.at[:, pl.ds(N - 1 if dy > 0 else 0, 1), :]
                dst = pb.at[pl.ds(1, N), pl.ds(3 if dy > 0 else 4 + N, 1), :]
        else:
            at = 12 + DIRS.index(d)
            wide = 14 if dx == 0 or dy == 0 else 13
            sx, tx = span(dx, wide, XO)
            sy, ty = span(dy, wide, YO)
            nx = wide if dx else N
            ny = wide if dy else N
            src = rb.at[pl.ds(sx, nx), pl.ds(sy, ny), :]
            dst = rb.at[pl.ds(tx, nx), pl.ds(ty, ny), :]
        return pltpu.make_async_remote_copy(
            src_ref=src, dst_ref=dst, send_sem=send.at[at], recv_sem=recv.at[at],
            device_id=device(d), device_id_type=MESH)

    def start(kind, dirs):
        for d in dirs:
            @pl.when(there(d))
            def _():
                message(kind, d).start()

    def arrive(kind, dirs):
        for d in dirs:
            @pl.when(there(back(d)))
            def _():
                message(kind, d).wait_recv()

    def sent(kind, dirs):
        for d in dirs:
            @pl.when(there(d))
            def _():
                message(kind, d).wait_send()

    start(1, SIDES)
    start(0, DIRS)

    load_t.wait()
    half = 0.5 * tb[...]
    lane = lax.broadcasted_iota(jnp.int32, (16, DEPTH), 1)
    up = jnp.where(lane < DEPTH - 1, pltpu.roll(half, DEPTH - 1, 1), 0.0)
    down = jnp.where(lane > 0, pltpu.roll(half, 1, 1), 0.0)
    wup = jnp.where(lane < DEPTH - 1, half + up, 0.0)
    vert = 6.0 * half + (up + down)
    wide = jnp.concatenate([half, wup, vert], axis=1)
    hi = wide.astype(jnp.bfloat16)
    rest = wide - hi.astype(jnp.float32)
    mid = rest.astype(jnp.bfloat16)
    low = (rest - mid.astype(jnp.float32)).astype(jnp.bfloat16)
    table = jnp.concatenate(
        [hi, mid, low, jnp.zeros((DEPTH - 48, 3 * DEPTH), jnp.bfloat16)], axis=0)

    def tags(block):
        pad = jnp.full((N, DEPTH - 3 * N), -1, jnp.int32)
        return jnp.concatenate([block.T, pad], axis=1)

    def coefficients(xs, y0, ny):
        lanes = lax.broadcasted_iota(jnp.int32, (ny, DEPTH), 1)
        slot = jnp.where(lanes < 48, lanes & 15, -9)
        at = pl.ds(y0, ny)
        tag = lt[at, :]
        hits = []
        for x in xs:
            c = x + N - XO
            hit = jnp.broadcast_to(tag[:, c:c + 1], (ny, DEPTH)) == slot
            hits.append(jnp.where(hit, 1.0, 0.0))
        onehot = jnp.concatenate(hits, axis=0).astype(jnp.bfloat16)
        out = jnp.dot(onehot, table, preferred_element_type=jnp.float32)
        for n, x in enumerate(xs):
            part = out[n * ny:(n + 1) * ny]
            s_ref[x, at, :] = part[:, :DEPTH]
            w_ref[x, at, :] = part[:, DEPTH:2 * DEPTH]
            k_ref[x, at, :] = part[:, 2 * DEPTH:]

    own_x = list(range(XO, XO + N))
    load_l.wait()
    none = jnp.full((N, N), -1, jnp.int32)
    lt[pl.ds(20, N), :] = tags(jnp.concatenate([none, lb[1, pl.ds(N, N), :], none], axis=0))
    coefficients(own_x, 16, 40)

    arrive(0, DIRS)
    lt[pl.ds(0, 20), :] = tags(lb[0])[12:]
    lt[pl.ds(20, N), :] = tags(lb[1])
    lt[pl.ds(52, 20), :] = tags(lb[2])[:20]

    def vertical(weight, value):
        return weight * pltpu.roll(value, DEPTH - 1, 1) + pltpu.roll(weight * value, 1, 1)

    for part in (range(0, XO), range(XO + N, NXF)):
        coefficients(list(part), 0, NYF)
    coefficients(own_x, 0, 24)
    coefficients(own_x, 48, 24)

    load_p.wait()
    load_s.wait()
    arrive(1, SIDES)

    @pl.loop(0, N)
    def _(x):
        fx = x + XO
        own = pl.ds(YO, N)
        s = s_ref[fx, own, :]
        sn = [s_ref[fx - 1, own, :], s_ref[fx + 1, own, :],
              s_ref[fx, pl.ds(YO - 1, N), :], s_ref[fx, pl.ds(YO + 1, N), :]]
        p = pb[x + 1, pl.ds(4, N), :]
        pn = [pb[x, pl.ds(4, N), :], pb[x + 2, pl.ds(4, N), :],
              pb[x + 1, pl.ds(3, N), :], pb[x + 1, pl.ds(5, N), :]]
        flow = (s + sn[0]) * (p - pn[0])
        for i in range(1, 4):
            flow = flow + (s + sn[i]) * (p - pn[i])
        both = k_ref[fx, own, :] - 4.0 * s
        flow = flow + (both * p - vertical(w_ref[fx, own, :], p))
        rb[fx, own, :] = sb[x] - flow

    start(2, DIRS)
    @pl.loop(4, NXF - 4)
    def _(x):
        at = pl.ds(4, 64)
        s = s_ref[x, at, :]
        diag = (k_ref[x, at, :] + (s_ref[x - 4, at, :] + s_ref[x + 4, at, :])
                + (s_ref[x, pl.ds(0, 64), :] + s_ref[x, pl.ds(8, 64), :]))
        k_ref[x, at, :] = jnp.where(s > 0.0, 0.8 / diag, 0.0)

    arrive(2, DIRS)

    sent(0, DIRS)
    sent(1, SIDES)
    sent(2, DIRS)


def relax(s_ref, w_ref, k_ref, rb, res_hbm, cor_hbm, ua, pa, ub, qb, uc, ob, local):
    out_r = pltpu.make_async_copy(rb.at[pl.ds(XO, N), pl.ds(YO, N), :], res_hbm, local.at[0])
    out_r.start()

    def vertical(weight, value):
        return weight * pltpu.roll(value, DEPTH - 1, 1) + pltpu.roll(weight * value, 1, 1)

    @pl.loop(0, (NXF - 8) // 2)
    def _(i):
        at = pl.ds(4, 64)
        for x in (4 + 2 * i, 5 + 2 * i):
            mean = (0.5 * rb[x, at, :]
                    + 0.125 * (rb[x - 1, at, :] + rb[x + 1, at, :]
                               + rb[x, pl.ds(3, 64), :] + rb[x, pl.ds(5, 64), :]))
            u = k_ref[x, at, :] * mean
            ua[x, at, :] = u
            pa[x, at, :] = s_ref[x, at, :] * u

    def sweep(first, u_in, p_in, u_out, p_out, base):
        y0, ny = first, NYF - 2 * first
        at = pl.ds(y0, ny)
        lo = pl.ds(y0 - 4, ny)
        hi_ = pl.ds(y0 + 4, ny)

        def row(x):
            s = s_ref[x, at, :]
            u = u_in[x, at, :]
            un = (u_in[x - 4, at, :] + u_in[x + 4, at, :]
                  + u_in[x, lo, :] + u_in[x, hi_, :])
            pn = (p_in[x - 4, at, :] + p_in[x + 4, at, :]
                  + p_in[x, lo, :] + p_in[x, hi_, :])
            total = s * un + pn + vertical(w_ref[x, at, :], u)
            new = base[x, at, :] + 0.2 * u + k_ref[x, at, :] * total
            return s, new

        @pl.loop(0, (NXF - 2 * first) // 2)
        def _(i):
            xs = (first + 2 * i, first + 2 * i + 1)
            out = [row(x) for x in xs]
            for x, (s, new) in zip(xs, out):
                u_out[x, at, :] = new
                if p_out is not None:
                    p_out[x, at, :] = s * new

    sweep(8, ua, pa, ub, qb, ua)
    sweep(12, ub, qb, uc, pa, ua)
    sweep(16, uc, pa, ub, None, ua)

    @pl.loop(0, N)
    def _(x):
        fx = x + XO
        at = pl.ds(YO, N)
        ob[x] = (0.5 * ub[fx, at, :]
                 + 0.125 * (ub[fx - 1, at, :] + ub[fx + 1, at, :]
                            + ub[fx, pl.ds(YO - 1, N), :] + ub[fx, pl.ds(YO + 1, N), :]))

    out_c = pltpu.make_async_copy(ob, cor_hbm, local.at[1])
    out_c.start()
    out_r.wait()
    out_c.wait()


def per_device(pressure, source, labels, region_table):
    hbm = pl.BlockSpec(memory_space=pltpu.HBM)
    vmem = pl.BlockSpec(memory_space=pltpu.VMEM)
    own = jax.ShapeDtypeStruct((N, N, DEPTH), jnp.float32)
    field = pltpu.VMEM((NXF, NYF, DEPTH), jnp.float32)
    fields = pl.pallas_call(
        exchange,
        out_shape=(field,) * 4,
        in_specs=[hbm] * 4,
        out_specs=(vmem,) * 4,
        scratch_shapes=[
            pltpu.VMEM((N + 2, 40, DEPTH), jnp.float32),
            pltpu.VMEM((N, N, DEPTH), jnp.float32),
            pltpu.VMEM((16, DEPTH), jnp.float32),
            pltpu.VMEM((3, 3 * N, N), jnp.int32),
            pltpu.VMEM((NYF, DEPTH), jnp.int32),
            pltpu.SemaphoreType.DMA((20,)),
            pltpu.SemaphoreType.DMA((20,)),
            pltpu.SemaphoreType.DMA((4,)),
        ],
        compiler_params=pltpu.CompilerParams(
            collective_id=0, has_side_effects=True, vmem_limit_bytes=24 << 20),
        name="exchange",
    )(*[pltpu.with_memory_space_constraint(a, pltpu.HBM)
        for a in (pressure, source, labels, region_table)])
    return pl.pallas_call(
        relax,
        out_shape=(own, own),
        in_specs=[vmem] * 4,
        out_specs=(hbm, hbm),
        scratch_shapes=[field] * 5 + [
            pltpu.VMEM((N, N, DEPTH), jnp.float32),
            pltpu.SemaphoreType.DMA((2,)),
        ],
        compiler_params=pltpu.CompilerParams(vmem_limit_bytes=24 << 20),
        name="relax",
    )(*fields)


def solution(mesh):
    placed = (P("space", "group", None), P("space", "group", None), P("space", "group"), P())
    return jax.shard_map(
        per_device,
        mesh=mesh,
        in_specs=placed,
        out_specs=(P("space", "group", None), P("space", "group", None)),
        check_vma=False,
    )
```

```python
import jax
import jax.numpy as jnp
from jax import lax
from jax.experimental import pallas as pl
from jax.experimental.pallas import tpu as pltpu
from jax.sharding import PartitionSpec as P

MESH = pl.DeviceIdType.MESH
N = 32
DEPTH = 128
XO, YO = 17, 20
NXF, NYF = 66, 72
R1, R2, R3 = 10, 7, 7
DIRS = [(dx, dy) for dx in (-1, 0, 1) for dy in (-1, 0, 1) if (dx, dy) != (0, 0)]
SIDES = [(-1, 0), (1, 0), (0, -1), (0, 1)]


def span(step, width, origin):
    if step == 1:
        return origin + N - width, origin - width
    if step == -1:
        return origin, origin + N
    return origin, origin


def exchange(p_hbm, src_hbm, lab_hbm, tab_hbm, s_ref, w_ref, k_ref, rb,
             pb, sb, tb, lb, lt, hx, hy, send, recv, local):
    groups = lax.axis_size("group")
    spaces = lax.axis_size("space")
    gi = lax.axis_index("group")
    si = lax.axis_index("space")

    def there(d):
        dx, dy = d
        ok = None
        if dx == 1:
            ok = si < spaces - 1
        elif dx == -1:
            ok = si > 0
        if dy:
            okg = gi < groups - 1 if dy == 1 else gi > 0
            ok = okg if ok is None else jnp.logical_and(ok, okg)
        return ok

    def back(d):
        return (-d[0], -d[1])

    def device(d):
        return (gi + d[1], si + d[0])

    load_p = pltpu.make_async_copy(p_hbm, pb.at[pl.ds(1, N), pl.ds(4, N), :], local.at[0])
    load_s = pltpu.make_async_copy(src_hbm, sb, local.at[1])
    load_l = pltpu.make_async_copy(lab_hbm, lb.at[1, pl.ds(N, N), :], local.at[2])
    load_t = pltpu.make_async_copy(tab_hbm, tb, local.at[3])
    load_l.start()
    load_t.start()
    load_p.start()
    load_s.start()

    barrier = pltpu.get_barrier_semaphore()
    count = jnp.int32(0)
    for d in DIRS:
        ok = there(d)
        count = count + ok.astype(jnp.int32)

        @pl.when(ok)
        def _():
            pl.semaphore_signal(barrier, 1, device_id=device(d), device_id_type=MESH)

    for d in DIRS:
        @pl.when(jnp.logical_not(there(d)))
        def _():
            dx, dy = d
            lb[1 + dy, pl.ds(N * (1 + dx), N), :] = jnp.full((N, N), -1, jnp.int32)

    for d in SIDES:
        @pl.when(jnp.logical_not(there(d)))
        def _():
            dx, dy = d
            if dx:
                r0 = XO - 14 if dx < 0 else XO + N

                @pl.loop(0, 14)
                def _(i):
                    rb[r0 + i] = jnp.zeros((NYF, DEPTH), jnp.float32)
            else:
                c0 = YO - 14 if dy < 0 else YO + N

                @pl.loop(XO - 14, XO + N + 14)
                def _(i):
                    rb[i, pl.ds(c0, 14), :] = jnp.zeros((14, DEPTH), jnp.float32)

    pl.semaphore_wait(barrier, count)

    def message(kind, d):
        dx, dy = d
        if kind == 0:
            at = DIRS.index(d)
            src = lab_hbm
            dst = lb.at[1 - dy, pl.ds(N * (1 - dx), N), :]
        elif kind == 1:
            at = 8 + SIDES.index(d)
            if dx:
                src = p_hbm.at[N - 1 if dx > 0 else 0]
                dst = hx.at[0 if dx > 0 else 1]
            else:
                src = p_hbm.at[:, N - 1 if dy > 0 else 0, :]
                dst = hy.at[0 if dy > 0 else 1]
        else:
            at = 12 + DIRS.index(d)
            wide = 14 if dx == 0 or dy == 0 else 13
            sx, tx = span(dx, wide, XO)
            sy, ty = span(dy, wide, YO)
            nx = wide if dx else N
            ny = wide if dy else N
            src = rb.at[pl.ds(sx, nx), pl.ds(sy, ny), :]
            dst = rb.at[pl.ds(tx, nx), pl.ds(ty, ny), :]
        return pltpu.make_async_remote_copy(
            src_ref=src, dst_ref=dst, send_sem=send.at[at], recv_sem=recv.at[at],
            device_id=device(d), device_id_type=MESH)

    def start(kind, dirs):
        for d in dirs:
            @pl.when(there(d))
            def _():
                message(kind, d).start()

    def arrive(kind, dirs):
        for d in dirs:
            @pl.when(there(back(d)))
            def _():
                message(kind, d).wait_recv()

    def sent(kind, dirs):
        for d in dirs:
            @pl.when(there(d))
            def _():
                message(kind, d).wait_send()

    start(1, SIDES)
    start(0, DIRS)

    load_t.wait()
    half = 0.5 * tb[...]
    lane = lax.broadcasted_iota(jnp.int32, (16, DEPTH), 1)
    up = jnp.where(lane < DEPTH - 1, pltpu.roll(half, DEPTH - 1, 1), 0.0)
    down = jnp.where(lane > 0, pltpu.roll(half, 1, 1), 0.0)
    wup = jnp.where(lane < DEPTH - 1, half + up, 0.0)
    vert = 6.0 * half + (up + down)
    wide = jnp.concatenate([half, wup, vert], axis=1)
    hi = wide.astype(jnp.bfloat16)
    rest = wide - hi.astype(jnp.float32)
    mid = rest.astype(jnp.bfloat16)
    low = (rest - mid.astype(jnp.float32)).astype(jnp.bfloat16)
    table = jnp.concatenate(
        [hi, mid, low, jnp.zeros((DEPTH - 48, 3 * DEPTH), jnp.bfloat16)], axis=0)

    def tags(block):
        pad = jnp.full((N, DEPTH - 3 * N), -1, jnp.int32)
        return jnp.concatenate([block.T, pad], axis=1)

    def coefficients(xs, y0, ny):
        lanes = lax.broadcasted_iota(jnp.int32, (ny, DEPTH), 1)
        slot = jnp.where(lanes < 48, lanes & 15, -9)
        at = pl.ds(y0, ny)
        tag = lt[at, :]
        hits = []
        for x in xs:
            c = x + N - XO
            hit = jnp.broadcast_to(tag[:, c:c + 1], (ny, DEPTH)) == slot
            hits.append(jnp.where(hit, 1.0, 0.0))
        onehot = jnp.concatenate(hits, axis=0).astype(jnp.bfloat16)
        out = jnp.dot(onehot, table, preferred_element_type=jnp.float32)
        for n, x in enumerate(xs):
            part = out[n * ny:(n + 1) * ny]
            s_ref[x, at, :] = part[:, :DEPTH]
            w_ref[x, at, :] = part[:, DEPTH:2 * DEPTH]
            k_ref[x, at, :] = part[:, 2 * DEPTH:]

    own_x = list(range(XO, XO + N))
    load_l.wait()
    none = jnp.full((N, N), -1, jnp.int32)
    lt[...] = jnp.full((NYF, DEPTH), -1, jnp.int32)
    lt[pl.ds(20, N), :] = tags(jnp.concatenate([none, lb[1, pl.ds(N, N), :], none], axis=0))
    coefficients(own_x, 16, 40)

    def vertical(weight, value):
        return weight * pltpu.roll(value, DEPTH - 1, 1) + pltpu.roll(weight * value, 1, 1)

    zero = jnp.zeros((N, DEPTH), jnp.float32)
    pb[0, pl.ds(4, N), :] = zero
    pb[N + 1, pl.ds(4, N), :] = zero
    s_ref[XO - 1, pl.ds(YO, N), :] = zero
    s_ref[XO + N, pl.ds(YO, N), :] = zero
    own = pl.ds(YO, N)
    load_p.wait()
    load_s.wait()
    pb[pl.ds(1, N), 3, :] = zero
    pb[pl.ds(1, N), 4 + N, :] = zero

    @pl.loop(0, N // 2)
    def _(i):
        out = []
        for x in (2 * i, 2 * i + 1):
            fx = x + XO
            s = s_ref[fx, own, :]
            sn = [s_ref[fx - 1, own, :], s_ref[fx + 1, own, :],
                  s_ref[fx, pl.ds(YO - 1, N), :], s_ref[fx, pl.ds(YO + 1, N), :]]
            p = pb[x + 1, pl.ds(4, N), :]
            pn = [pb[x, pl.ds(4, N), :], pb[x + 2, pl.ds(4, N), :],
                  pb[x + 1, pl.ds(3, N), :], pb[x + 1, pl.ds(5, N), :]]
            flow = (s + sn[0]) * (p - pn[0])
            for n in range(1, 4):
                flow = flow + (s + sn[n]) * (p - pn[n])
            both = k_ref[fx, own, :] - 4.0 * s
            flow = flow + (both * p - vertical(w_ref[fx, own, :], p))
            out.append(sb[x] - flow)
        for n in (0, 1):
            rb[2 * i + n + XO, own, :] = out[n]

    arrive(0, DIRS)
    lt[pl.ds(0, 20), :] = tags(lb[0])[12:]
    lt[pl.ds(20, N), :] = tags(lb[1])
    lt[pl.ds(52, 20), :] = tags(lb[2])[:20]

    coefficients([XO - 1, XO + N], 16, 40)
    coefficients(own_x, 16, 8)
    coefficients(own_x, 48, 8)

    def outward(s, sn, p, pn):
        return (s + sn) * (p - pn) - s * p

    for d in SIDES:
        @pl.when(there(d))
        def _():
            dx, dy = d
            message(1, back(d)).wait_recv()
            if dx:
                f = XO if dx < 0 else XO + N - 1
                rb[f, own, :] = rb[f, own, :] - outward(
                    s_ref[f, own, :], s_ref[f + dx, own, :],
                    pb[f - XO + 1, pl.ds(4, N), :], hx[0 if dx < 0 else 1])
            else:
                f = YO if dy < 0 else YO + N - 1
                xs = pl.ds(XO, N)
                rb[xs, f, :] = rb[xs, f, :] - outward(
                    s_ref[xs, f, :], s_ref[xs, f + dy, :],
                    pb[pl.ds(1, N), f - YO + 4, :], hy[0 if dy < 0 else 1])

    start(2, [(0, -1), (0, 1), (-1, -1), (-1, 1), (1, -1), (1, 1), (-1, 0), (1, 0)])

    for part in (range(0, XO - 1), range(XO + N + 1, NXF)):
        coefficients(list(part), 0, NYF)
    coefficients([XO - 1, XO + N], 0, 16)
    coefficients([XO - 1, XO + N], 56, 16)
    coefficients(own_x, 0, 16)
    coefficients(own_x, 56, 16)

    @pl.loop(4, NXF - 4)
    def _(x):
        at = pl.ds(4, 64)
        s = s_ref[x, at, :]
        diag = (k_ref[x, at, :] + (s_ref[x - 4, at, :] + s_ref[x + 4, at, :])
                + (s_ref[x, pl.ds(0, 64), :] + s_ref[x, pl.ds(8, 64), :]))
        k_ref[x, at, :] = jnp.where(s > 0.0, 0.8 / diag, 0.0)

    arrive(2, DIRS)

    sent(0, DIRS)
    sent(1, SIDES)
    sent(2, DIRS)


def relax(s_ref, w_ref, k_ref, rb, res_hbm, cor_hbm, ua, pa, ub, qb, uc, ob, local):
    out_r = pltpu.make_async_copy(rb.at[pl.ds(XO, N), pl.ds(YO, N), :], res_hbm, local.at[0])
    out_r.start()

    def vertical(weight, value):
        return weight * pltpu.roll(value, DEPTH - 1, 1) + pltpu.roll(weight * value, 1, 1)

    @pl.loop(0, (NXF - 8) // 2)
    def _(i):
        at = pl.ds(4, 64)
        for x in (4 + 2 * i, 5 + 2 * i):
            mean = (0.5 * rb[x, at, :]
                    + 0.125 * (rb[x - 1, at, :] + rb[x + 1, at, :]
                               + rb[x, pl.ds(3, 64), :] + rb[x, pl.ds(5, 64), :]))
            u = k_ref[x, at, :] * mean
            ua[x, at, :] = u
            pa[x, at, :] = s_ref[x, at, :] * u

    def sweep(rows, first, u_in, p_in, u_out, p_out, base):
        y0, ny = first, NYF - 2 * first
        at = pl.ds(y0, ny)
        lo = pl.ds(y0 - 4, ny)
        hi_ = pl.ds(y0 + 4, ny)

        def column(x):
            return vertical(w_ref[x, at, :], u_in[x, at, :])

        def row(x, column):
            s = s_ref[x, at, :]
            u = u_in[x, at, :]
            un = (u_in[x - 4, at, :] + u_in[x + 4, at, :]
                  + u_in[x, lo, :] + u_in[x, hi_, :])
            pn = (p_in[x - 4, at, :] + p_in[x + 4, at, :]
                  + p_in[x, lo, :] + p_in[x, hi_, :])
            new = base[x, at, :] + 0.2 * u + k_ref[x, at, :] * (s * un + pn + column)
            return s, new

        @pl.loop(0, pl.cdiv(NXF - 2 * first, rows))
        def _(i):
            x0 = first + rows * i
            out = [row(x0 + n, column(x0 + n)) for n in range(rows)]
            for n, (s, new) in enumerate(out):
                u_out[x0 + n, at, :] = new
                if p_out is not None:
                    p_out[x0 + n, at, :] = s * new

    sweep(R1, 8, ua, pa, ub, qb, ua)
    sweep(R2, 12, ub, qb, uc, pa, ua)
    sweep(R3, 16, uc, pa, ub, None, ua)

    @pl.loop(0, N)
    def _(x):
        fx = x + XO
        at = pl.ds(YO, N)
        ob[x] = (0.5 * ub[fx, at, :]
                 + 0.125 * (ub[fx - 1, at, :] + ub[fx + 1, at, :]
                            + ub[fx, pl.ds(YO - 1, N), :] + ub[fx, pl.ds(YO + 1, N), :]))

    out_c = pltpu.make_async_copy(ob, cor_hbm, local.at[1])
    out_c.start()
    out_r.wait()
    out_c.wait()


def per_device(pressure, source, labels, region_table):
    hbm = pl.BlockSpec(memory_space=pltpu.HBM)
    vmem = pl.BlockSpec(memory_space=pltpu.VMEM)
    own = jax.ShapeDtypeStruct((N, N, DEPTH), jnp.float32)
    field = pltpu.VMEM((NXF, NYF, DEPTH), jnp.float32)
    fields = pl.pallas_call(
        exchange,
        out_shape=(field,) * 4,
        in_specs=[hbm] * 4,
        out_specs=(vmem,) * 4,
        scratch_shapes=[
            pltpu.VMEM((N + 2, 40, DEPTH), jnp.float32),
            pltpu.VMEM((N, N, DEPTH), jnp.float32),
            pltpu.VMEM((16, DEPTH), jnp.float32),
            pltpu.VMEM((3, 3 * N, N), jnp.int32),
            pltpu.VMEM((NYF, DEPTH), jnp.int32),
            pltpu.VMEM((2, N, DEPTH), jnp.float32),
            pltpu.VMEM((2, N, DEPTH), jnp.float32),
            pltpu.SemaphoreType.DMA((20,)),
            pltpu.SemaphoreType.DMA((20,)),
            pltpu.SemaphoreType.DMA((4,)),
        ],
        compiler_params=pltpu.CompilerParams(
            collective_id=0, has_side_effects=True, vmem_limit_bytes=24 << 20),
        name="exchange",
    )(*[pltpu.with_memory_space_constraint(a, pltpu.HBM)
        for a in (pressure, source, labels, region_table)])
    return pl.pallas_call(
        relax,
        out_shape=(own, own),
        in_specs=[vmem] * 4,
        out_specs=(hbm, hbm),
        scratch_shapes=[field] * 5 + [
            pltpu.VMEM((N, N, DEPTH), jnp.float32),
            pltpu.SemaphoreType.DMA((2,)),
        ],
        compiler_params=pltpu.CompilerParams(vmem_limit_bytes=24 << 20),
        name="relax",
    )(*fields)


def solution(mesh):
    placed = (P("space", "group", None), P("space", "group", None), P("space", "group"), P())
    return jax.shard_map(
        per_device,
        mesh=mesh,
        in_specs=placed,
        out_specs=(P("space", "group", None), P("space", "group", None)),
        check_vma=False,
    )
```

```python
import jax
import jax.numpy as jnp
from jax import lax
from jax.experimental import pallas as pl
from jax.experimental.pallas import tpu as pltpu
from jax.sharding import PartitionSpec as P

MESH = pl.DeviceIdType.MESH
N = 32
DEPTH = 128
XO, YO = 17, 20
NXF, NYF = 66, 72
R1, R2, R3 = 50, 42, 34
DIRS = [(dx, dy) for dx in (-1, 0, 1) for dy in (-1, 0, 1) if (dx, dy) != (0, 0)]
ORDER = [(0, -1), (0, 1), (-1, 0), (1, 0), (-1, -1), (-1, 1), (1, -1), (1, 1)]
SIDES = [(-1, 0), (1, 0), (0, -1), (0, 1)]


def pieces(d, edge):
    dx, dy = d
    if dy == 0:
        if not edge:
            return [((2, 14), (1, N - 2))]
        return [((1, 1), (0, N - 1)), ((2, 14), (0, 0)), ((2, 14), (N - 1, N - 1))]
    if dx == 0:
        if not edge:
            return [((1, N - 2), (2, 14))]
        return [((0, N - 1), (1, 1)), ((0, 0), (2, 14)), ((N - 1, N - 1), (2, 14))]
    if not edge:
        return [((2, 6), (2, 12)), ((7, 12), (2, 6))]
    return [((1, 1), (1, 13)), ((2, 13), (1, 1))]


def span(step, lo, hi):
    if step == 1:
        return N - hi, hi - lo + 1
    if step == -1:
        return lo - 1, hi - lo + 1
    return lo, hi - lo + 1


PARTS = [(d, edge, n) for edge in (False, True) for d in DIRS for n in range(len(pieces(d, edge)))]
COPIES = 12 + len(PARTS)


def exchange(p_hbm, src_hbm, lab_hbm, tab_hbm, s_ref, w_ref, k_ref, rb,
             pb, sb, tb, lb, lt, hx, hy, send, recv, local):
    groups = lax.axis_size("group")
    spaces = lax.axis_size("space")
    gi = lax.axis_index("group")
    si = lax.axis_index("space")

    def there(d):
        dx, dy = d
        ok = None
        if dx == 1:
            ok = si < spaces - 1
        elif dx == -1:
            ok = si > 0
        if dy:
            okg = gi < groups - 1 if dy == 1 else gi > 0
            ok = okg if ok is None else jnp.logical_and(ok, okg)
        return ok

    def back(d):
        return (-d[0], -d[1])

    def device(d):
        return (gi + d[1], si + d[0])

    load_p = pltpu.make_async_copy(p_hbm, pb.at[pl.ds(1, N), pl.ds(4, N), :], local.at[0])
    load_s = pltpu.make_async_copy(src_hbm, sb, local.at[1])
    load_l = pltpu.make_async_copy(lab_hbm, lb.at[1, pl.ds(N, N), :], local.at[2])
    load_t = pltpu.make_async_copy(tab_hbm, tb, local.at[3])
    load_l.start()
    load_t.start()
    load_p.start()
    load_s.start()

    barrier = pltpu.get_barrier_semaphore()
    count = jnp.int32(0)
    for d in DIRS:
        ok = there(d)
        count = count + ok.astype(jnp.int32)

        @pl.when(ok)
        def _():
            pl.semaphore_signal(barrier, 1, device_id=device(d), device_id_type=MESH)

    for d in DIRS:
        @pl.when(jnp.logical_not(there(d)))
        def _():
            dx, dy = d
            lb[1 + dy, pl.ds(N * (1 + dx), N), :] = jnp.full((N, N), -1, jnp.int32)

    for d in SIDES:
        @pl.when(jnp.logical_not(there(d)))
        def _():
            dx, dy = d
            if dx:
                r0 = XO - 14 if dx < 0 else XO + N

                @pl.loop(0, 14)
                def _(i):
                    rb[r0 + i] = jnp.zeros((NYF, DEPTH), jnp.float32)
            else:
                c0 = YO - 14 if dy < 0 else YO + N

                @pl.loop(XO - 14, XO + N + 14)
                def _(i):
                    rb[i, pl.ds(c0, 14), :] = jnp.zeros((14, DEPTH), jnp.float32)

    pl.semaphore_wait(barrier, count)

    def remote(src, dst, at, d):
        return pltpu.make_async_remote_copy(
            src_ref=src, dst_ref=dst, send_sem=send.at[at], recv_sem=recv.at[at],
            device_id=device(d), device_id_type=MESH)

    def messages(kind, d):
        dx, dy = d
        if kind == 0:
            r0, rows = (15, 17) if dx > 0 else (0, 17) if dx < 0 else (0, N)
            return [remote(lab_hbm.at[pl.ds(r0, rows), :],
                           lb.at[1 - dy, pl.ds(N * (1 - dx) + r0, rows), :], DIRS.index(d), d)]
        if kind == 1:
            at = 8 + SIDES.index(d)
            if dx:
                return [remote(p_hbm.at[N - 1 if dx > 0 else 0], hx.at[0 if dx > 0 else 1], at, d)]
            return [remote(p_hbm.at[:, N - 1 if dy > 0 else 0, :], hy.at[0 if dy > 0 else 1], at, d)]
        edge = kind == 3
        out = []
        for n, (rows, cols) in enumerate(pieces(d, edge)):
            x, nx = span(dx, *rows)
            y, ny = span(dy, *cols)
            x = x + XO
            y = y + YO
            out.append(remote(rb.at[pl.ds(x, nx), pl.ds(y, ny), :],
                              rb.at[pl.ds(x - N * dx, nx), pl.ds(y - N * dy, ny), :],
                              12 + PARTS.index((d, edge, n)), d))
        return out

    def start(kinds, dirs):
        for d in dirs:
            @pl.when(there(d))
            def _():
                for kind in kinds:
                    for m in messages(kind, d):
                        m.start()

    def arrive(kinds, dirs):
        for d in dirs:
            @pl.when(there(back(d)))
            def _():
                for kind in kinds:
                    for m in messages(kind, d):
                        m.wait_recv()

    def sent(kinds, dirs):
        for d in dirs:
            @pl.when(there(d))
            def _():
                for kind in kinds:
                    for m in messages(kind, d):
                        m.wait_send()

    start([1], SIDES)
    start([0], DIRS)

    load_t.wait()
    half = 0.5 * tb[...]
    lane = lax.broadcasted_iota(jnp.int32, (16, DEPTH), 1)
    up = jnp.where(lane < DEPTH - 1, pltpu.roll(half, DEPTH - 1, 1), 0.0)
    down = jnp.where(lane > 0, pltpu.roll(half, 1, 1), 0.0)
    wup = jnp.where(lane < DEPTH - 1, half + up, 0.0)
    vert = 6.0 * half + (up + down)
    wide = jnp.concatenate([half, wup, vert], axis=1)
    hi = wide.astype(jnp.bfloat16)
    rest = wide - hi.astype(jnp.float32)
    mid = rest.astype(jnp.bfloat16)
    low = (rest - mid.astype(jnp.float32)).astype(jnp.bfloat16)
    table = jnp.concatenate(
        [hi, mid, low, jnp.zeros((DEPTH - 48, 3 * DEPTH), jnp.bfloat16)], axis=0)

    def tags(block):
        pad = jnp.full((N, DEPTH - 3 * N), -1, jnp.int32)
        return jnp.concatenate([block.T, pad], axis=1)

    def coefficients(xs, y0, ny):
        lanes = lax.broadcasted_iota(jnp.int32, (ny, DEPTH), 1)
        slot = jnp.where(lanes < 48, lanes & 15, -9)
        at = pl.ds(y0, ny)
        tag = lt[at, :]
        hits = []
        for x in xs:
            c = x + N - XO
            hit = jnp.broadcast_to(tag[:, c:c + 1], (ny, DEPTH)) == slot
            hits.append(jnp.where(hit, 1.0, 0.0))
        onehot = jnp.concatenate(hits, axis=0).astype(jnp.bfloat16)
        out = jnp.dot(onehot, table, preferred_element_type=jnp.float32)
        for n, x in enumerate(xs):
            part = out[n * ny:(n + 1) * ny]
            s_ref[x, at, :] = part[:, :DEPTH]
            w_ref[x, at, :] = part[:, DEPTH:2 * DEPTH]
            k_ref[x, at, :] = part[:, 2 * DEPTH:]

    own_x = list(range(XO, XO + N))
    load_l.wait()
    none = jnp.full((N, N), -1, jnp.int32)
    lt[...] = jnp.full((NYF, DEPTH), -1, jnp.int32)
    lt[pl.ds(20, N), :] = tags(jnp.concatenate([none, lb[1, pl.ds(N, N), :], none], axis=0))
    coefficients(own_x, 16, 40)

    def vertical(weight, value):
        return weight * pltpu.roll(value, DEPTH - 1, 1) + pltpu.roll(weight * value, 1, 1)

    zero = jnp.zeros((N, DEPTH), jnp.float32)
    pb[0, pl.ds(4, N), :] = zero
    pb[N + 1, pl.ds(4, N), :] = zero
    s_ref[XO - 1, pl.ds(YO, N), :] = zero
    s_ref[XO + N, pl.ds(YO, N), :] = zero
    own = pl.ds(YO, N)
    load_p.wait()
    load_s.wait()
    pb[pl.ds(1, N), 3, :] = zero
    pb[pl.ds(1, N), 4 + N, :] = zero

    @pl.loop(0, N // 8)
    def _(i):
        out = []
        for x in [8 * i + n for n in range(8)]:
            fx = x + XO
            s = s_ref[fx, own, :]
            sn = [s_ref[fx - 1, own, :], s_ref[fx + 1, own, :],
                  s_ref[fx, pl.ds(YO - 1, N), :], s_ref[fx, pl.ds(YO + 1, N), :]]
            p = pb[x + 1, pl.ds(4, N), :]
            pn = [pb[x, pl.ds(4, N), :], pb[x + 2, pl.ds(4, N), :],
                  pb[x + 1, pl.ds(3, N), :], pb[x + 1, pl.ds(5, N), :]]
            flow = (s + sn[0]) * (p - pn[0])
            for n in range(1, 4):
                flow = flow + (s + sn[n]) * (p - pn[n])
            both = k_ref[fx, own, :] - 4.0 * s
            flow = flow + (both * p - vertical(w_ref[fx, own, :], p))
            out.append(sb[x] - flow)
        for n in range(8):
            rb[8 * i + n + XO, own, :] = out[n]

    start([2], ORDER)
    arrive([0], DIRS)
    lt[pl.ds(0, 20), :] = tags(lb[0])[12:]
    lt[pl.ds(20, N), :] = tags(lb[1])
    lt[pl.ds(52, 20), :] = tags(lb[2])[:20]

    coefficients([XO - 1, XO + N], 16, 40)
    coefficients(own_x, 16, 8)
    coefficients(own_x, 48, 8)

    def outward(s, sn, p, pn):
        return (s + sn) * (p - pn) - s * p

    for d in SIDES:
        @pl.when(there(d))
        def _():
            dx, dy = d
            messages(1, back(d))[0].wait_recv()
            if dx:
                f = XO if dx < 0 else XO + N - 1
                rb[f, own, :] = rb[f, own, :] - outward(
                    s_ref[f, own, :], s_ref[f + dx, own, :],
                    pb[f - XO + 1, pl.ds(4, N), :], hx[0 if dx < 0 else 1])
            else:
                f = YO if dy < 0 else YO + N - 1
                xs = pl.ds(XO, N)
                rb[xs, f, :] = rb[xs, f, :] - outward(
                    s_ref[xs, f, :], s_ref[xs, f + dy, :],
                    pb[pl.ds(1, N), f - YO + 4, :], hy[0 if dy < 0 else 1])

    start([3], ORDER)

    for part in (range(0, XO - 1), range(XO + N + 1, NXF)):
        coefficients(list(part), 0, NYF)
    coefficients([XO - 1, XO + N], 0, 16)
    coefficients([XO - 1, XO + N], 56, 16)
    coefficients(own_x, 0, 16)
    coefficients(own_x, 56, 16)

    @pl.loop(4, NXF - 4)
    def _(x):
        at = pl.ds(4, 64)
        s = s_ref[x, at, :]
        diag = (k_ref[x, at, :] + (s_ref[x - 4, at, :] + s_ref[x + 4, at, :])
                + (s_ref[x, pl.ds(0, 64), :] + s_ref[x, pl.ds(8, 64), :]))
        k_ref[x, at, :] = jnp.where(s > 0.0, 0.8 / diag, 0.0)

    arrive([2, 3], DIRS)

    sent([1], SIDES)
    sent([0, 2, 3], DIRS)


def relax(s_ref, w_ref, k_ref, rb, res_hbm, cor_hbm, ua, pa, ub, qb, uc, ob, local):
    out_r = pltpu.make_async_copy(rb.at[pl.ds(XO, N), pl.ds(YO, N), :], res_hbm, local.at[0])
    out_r.start()

    def vertical(weight, value):
        return weight * pltpu.roll(value, DEPTH - 1, 1) + pltpu.roll(weight * value, 1, 1)

    @pl.loop(0, (NXF - 8) // 2)
    def _(i):
        at = pl.ds(4, 64)
        for x in (4 + 2 * i, 5 + 2 * i):
            mean = (0.5 * rb[x, at, :]
                    + 0.125 * (rb[x - 1, at, :] + rb[x + 1, at, :]
                               + rb[x, pl.ds(3, 64), :] + rb[x, pl.ds(5, 64), :]))
            u = k_ref[x, at, :] * mean
            ua[x, at, :] = u
            pa[x, at, :] = s_ref[x, at, :] * u

    def sweep(rows, first, u_in, p_in, u_out, p_out, base):
        y0, ny = first, NYF - 2 * first
        at = pl.ds(y0, ny)
        lo = pl.ds(y0 - 4, ny)
        hi_ = pl.ds(y0 + 4, ny)

        def column(x):
            return vertical(w_ref[x, at, :], u_in[x, at, :])

        def row(x, column):
            s = s_ref[x, at, :]
            u = u_in[x, at, :]
            un = (u_in[x - 4, at, :] + u_in[x + 4, at, :]
                  + u_in[x, lo, :] + u_in[x, hi_, :])
            pn = (p_in[x - 4, at, :] + p_in[x + 4, at, :]
                  + p_in[x, lo, :] + p_in[x, hi_, :])
            new = base[x, at, :] + 0.2 * u + k_ref[x, at, :] * (s * un + pn + column)
            return s, new

        @pl.loop(0, pl.cdiv(NXF - 2 * first, rows))
        def _(i):
            x0 = first + rows * i
            out = [row(x0 + n, column(x0 + n)) for n in range(rows)]
            for n, (s, new) in enumerate(out):
                u_out[x0 + n, at, :] = new
                if p_out is not None:
                    p_out[x0 + n, at, :] = s * new

    sweep(R1, 8, ua, pa, ub, qb, ua)
    sweep(R2, 12, ub, qb, uc, pa, ua)
    sweep(R3, 16, uc, pa, ub, None, ua)

    def out_c(c):
        rows = pl.ds(8 * c, 8)
        return pltpu.make_async_copy(ob.at[rows], cor_hbm.at[rows], local.at[1 + c])

    for c in range(4):
        @pl.loop(8 * c, 8 * c + 8, unroll=True)
        def _(x):
            fx = x + XO
            at = pl.ds(YO, N)
            ob[x] = (0.5 * ub[fx, at, :]
                     + 0.125 * (ub[fx - 1, at, :] + ub[fx + 1, at, :]
                                + ub[fx, pl.ds(YO - 1, N), :] + ub[fx, pl.ds(YO + 1, N), :]))

        out_c(c).start()
    out_r.wait()
    for c in range(4):
        out_c(c).wait()


def per_device(pressure, source, labels, region_table):
    hbm = pl.BlockSpec(memory_space=pltpu.HBM)
    vmem = pl.BlockSpec(memory_space=pltpu.VMEM)
    own = jax.ShapeDtypeStruct((N, N, DEPTH), jnp.float32)
    field = pltpu.VMEM((NXF, NYF, DEPTH), jnp.float32)
    fields = pl.pallas_call(
        exchange,
        out_shape=(field,) * 4,
        in_specs=[hbm] * 4,
        out_specs=(vmem,) * 4,
        scratch_shapes=[
            pltpu.VMEM((N + 2, 40, DEPTH), jnp.float32),
            pltpu.VMEM((N, N, DEPTH), jnp.float32),
            pltpu.VMEM((16, DEPTH), jnp.float32),
            pltpu.VMEM((3, 3 * N, N), jnp.int32),
            pltpu.VMEM((NYF, DEPTH), jnp.int32),
            pltpu.VMEM((2, N, DEPTH), jnp.float32),
            pltpu.VMEM((2, N, DEPTH), jnp.float32),
            pltpu.SemaphoreType.DMA((COPIES,)),
            pltpu.SemaphoreType.DMA((COPIES,)),
            pltpu.SemaphoreType.DMA((4,)),
        ],
        compiler_params=pltpu.CompilerParams(
            collective_id=0, has_side_effects=True, vmem_limit_bytes=24 << 20),
        name="exchange",
    )(*[pltpu.with_memory_space_constraint(a, pltpu.HBM)
        for a in (pressure, source, labels, region_table)])
    return pl.pallas_call(
        relax,
        out_shape=(own, own),
        in_specs=[vmem] * 4,
        out_specs=(hbm, hbm),
        scratch_shapes=[field] * 5 + [
            pltpu.VMEM((N, N, DEPTH), jnp.float32),
            pltpu.SemaphoreType.DMA((5,)),
        ],
        compiler_params=pltpu.CompilerParams(vmem_limit_bytes=24 << 20),
        name="relax",
    )(*fields)


def solution(mesh):
    placed = (P("space", "group", None), P("space", "group", None), P("space", "group"), P())
    return jax.shard_map(
        per_device,
        mesh=mesh,
        in_specs=placed,
        out_specs=(P("space", "group", None), P("space", "group", None)),
        check_vma=False,
    )
```

```python
import jax
import jax.numpy as jnp
from jax import lax
from jax.experimental import pallas as pl
from jax.experimental.pallas import tpu as pltpu
from jax.sharding import PartitionSpec as P

MESH = pl.DeviceIdType.MESH
N = 32
DEPTH = 128
XO, YO = 17, 20
NXF, NYF = 66, 72
DIRS = [(dx, dy) for dx in (-1, 0, 1) for dy in (-1, 0, 1) if (dx, dy) != (0, 0)]
ORDER = [(0, -1), (0, 1), (-1, -1), (-1, 1), (1, -1), (1, 1), (-1, 0), (1, 0)]
DIRS_X, DIRS_Y = [(-1, 0), (1, 0)], [(0, -1), (0, 1)]
DIRS_XY = [(-1, -1), (-1, 1), (1, -1), (1, 1)]
SIDES = DIRS_X + DIRS_Y


def pieces(d, stage):
    dx, dy = d
    if dy == 0:
        return [((1, 14), (1, N - 2))] if stage == (dx > 0) else []
    if dx == 0:
        return [((1, 15), (1, 14)) if stage == 0 else ((16, N - 2), (1, 14))]
    return [((2, 6), (2, 12)), ((7, 12), (2, 6))] if stage == (dx > 0) else []


def span(step, lo, hi):
    if step == 1:
        return N - hi, hi - lo + 1
    if step == -1:
        return lo - 1, hi - lo + 1
    return lo, hi - lo + 1


XSIDES, YSIDES, CORNERS = DIRS_X, DIRS_Y, DIRS_XY
KINDS = {0: DIRS, 1: SIDES, 2: DIRS, 3: DIRS, 4: YSIDES, 5: XSIDES, 6: CORNERS}
KEYS = [(kind, d, n) for kind, dirs in KINDS.items() for d in dirs
        for n in range(len(pieces(d, kind - 2)) if kind in (2, 3) else (1, 1, 0, 0, 2, 2, 3)[kind])]


def columns(reach, x):
    beyond = max(XO - x, x - (XO + N - 1), 1)
    side = reach - 4 * (-(-(beyond - 1) // 4))
    return YO - side - 3, -(-(N + 2 * side) // 8) * 8


def exchange(p_hbm, src_hbm, lab_hbm, tab_hbm, s_ref, w_ref, k_ref, rb,
             pb, sb, tb, lb, lt, hx, hy, ax, ay, bx, by, rx, cy, cc,
             send, recv, local):
    groups = lax.axis_size("group")
    spaces = lax.axis_size("space")
    gi = lax.axis_index("group")
    si = lax.axis_index("space")

    def there(d):
        dx, dy = d
        ok = None
        if dx == 1:
            ok = si < spaces - 1
        elif dx == -1:
            ok = si > 0
        if dy:
            okg = gi < groups - 1 if dy == 1 else gi > 0
            ok = okg if ok is None else jnp.logical_and(ok, okg)
        return ok

    def back(d):
        return (-d[0], -d[1])

    def device(d):
        return (gi + d[1], si + d[0])

    halves = ((0, 17), (17, 15))
    load_p = [pltpu.make_async_copy(p_hbm.at[pl.ds(a, n)], pb.at[pl.ds(1 + a, n), pl.ds(4, N), :],
                                    local.at[4 + h]) for h, (a, n) in enumerate(halves)]
    load_s = [pltpu.make_async_copy(src_hbm.at[pl.ds(a, n)], sb.at[pl.ds(a, n)],
                                    local.at[h]) for h, (a, n) in enumerate(halves)]
    load_l = pltpu.make_async_copy(lab_hbm, lb.at[1, pl.ds(N, N), :], local.at[2])
    load_t = pltpu.make_async_copy(tab_hbm, tb, local.at[3])
    load_l.start()
    load_t.start()
    for h in (0, 1):
        load_p[h].start()
        load_s[h].start()

    barrier = pltpu.get_barrier_semaphore()
    count = jnp.int32(0)
    for d in DIRS:
        ok = there(d)
        count = count + ok.astype(jnp.int32)

        @pl.when(ok)
        def _():
            pl.semaphore_signal(barrier, 1, device_id=device(d), device_id_type=MESH)

    for d in DIRS:
        @pl.when(jnp.logical_not(there(d)))
        def _():
            dx, dy = d
            lb[1 + dy, pl.ds(N * (1 + dx), N), :] = jnp.full((N, N), -1, jnp.int32)

    for d in SIDES:
        @pl.when(jnp.logical_not(there(d)))
        def _():
            dx, dy = d
            if dx:
                hx[int(dx > 0)] = jnp.zeros((N, DEPTH), jnp.float32)
                r0 = XO - 14 if dx < 0 else XO + N

                @pl.loop(0, 14)
                def _(i):
                    rb[r0 + i] = jnp.zeros((NYF, DEPTH), jnp.float32)
            else:
                hy[int(dy > 0)] = jnp.zeros((N, DEPTH), jnp.float32)
                c0 = YO - 14 if dy < 0 else YO + N

                @pl.loop(XO - 14, XO + N + 14)
                def _(i):
                    rb[i, pl.ds(c0, 14), :] = jnp.zeros((14, DEPTH), jnp.float32)

    def messages(kind, d):
        dx, dy = d
        ex, ey = int(dx > 0), int(dy > 0)
        last = N - 1
        if kind == 0:
            r0, rows = (15, 17) if dx > 0 else (0, 17) if dx < 0 else (0, N)
            ends = [(lab_hbm.at[pl.ds(r0, rows), :],
                     lb.at[1 - dy, pl.ds(N * (1 - dx) + r0, rows), :])]
        elif kind == 1:
            ends = [(p_hbm.at[last * ex], hx.at[1 - ex]) if dx
                    else (p_hbm.at[:, last * ey, :], hy.at[1 - ey])]
        elif kind in (2, 3):
            ends = []
            for rows, cols in pieces(d, kind - 2):
                x, nx = span(dx, *rows)
                y, ny = span(dy, *cols)
                x = x + XO
                y = y + YO
                ends.append((rb.at[pl.ds(x, nx), pl.ds(y, ny), :],
                             rb.at[pl.ds(x - N * dx, nx), pl.ds(y - N * dy, ny), :]))
        elif kind == 4:
            y = (N - 14) * ey
            ends = [(rx.at[e, pl.ds(y, 14), :],
                     rb.at[XO + last * e, pl.ds(YO + y - N * dy, 14), :]) for e in (0, 1)]
        elif kind == 5:
            x = (N - 14) * ex
            ends = [(cy.at[e, pl.ds(x, 14), :],
                     rb.at[pl.ds(XO + x - N * dx, 14), YO + last * e, :]) for e in (0, 1)]
        else:
            x, y = (N - 13 if ex else 1), (N - 13 if ey else 1)
            fx, fy = XO + last * ex - N * dx, YO + last * ey - N * dy
            ends = [(rx.at[ex, pl.ds(y, 12), :], rb.at[fx, pl.ds(YO + y - N * dy, 12), :]),
                    (cy.at[ey, pl.ds(x, 12), :], rb.at[pl.ds(XO + x - N * dx, 12), fy, :]),
                    (cc.at[2 * ex + ey], rb.at[fx, pl.ds(fy, 1), :])]
        return [pltpu.make_async_remote_copy(
            src_ref=src, dst_ref=dst, send_sem=send.at[KEYS.index((kind, d, n))],
            recv_sem=recv.at[KEYS.index((kind, d, n))], device_id=device(d), device_id_type=MESH)
            for n, (src, dst) in enumerate(ends)]

    def held(kinds, d):
        return [k for k in kinds if any(key[:2] == (k, d) for key in KEYS)]

    def start(kinds, dirs):
        for d in dirs:
            if not held(kinds, d):
                continue

            @pl.when(there(d))
            def _():
                for kind in held(kinds, d):
                    for m in messages(kind, d):
                        m.start()

    def arrive(kinds, dirs):
        for d in dirs:
            @pl.when(there(back(d)))
            def _():
                for kind in held(kinds, d):
                    for m in messages(kind, d):
                        m.wait_recv()

    def sent(kinds, dirs):
        for d in dirs:
            @pl.when(there(d))
            def _():
                for kind in held(kinds, d):
                    for m in messages(kind, d):
                        m.wait_send()


    load_t.wait()
    half = 0.5 * tb[...]
    lane = lax.broadcasted_iota(jnp.int32, (16, DEPTH), 1)
    up = jnp.where(lane < DEPTH - 1, pltpu.roll(half, DEPTH - 1, 1), 0.0)
    down = jnp.where(lane > 0, pltpu.roll(half, 1, 1), 0.0)
    wup = jnp.where(lane < DEPTH - 1, half + up, 0.0)
    vert = 6.0 * half + (up + down)
    wide = jnp.concatenate([half, wup, vert], axis=1)
    hi = wide.astype(jnp.bfloat16)
    rest = wide - hi.astype(jnp.float32)
    mid = rest.astype(jnp.bfloat16)
    low = (rest - mid.astype(jnp.float32)).astype(jnp.bfloat16)
    table = jnp.concatenate(
        [hi, mid, low, jnp.zeros((DEPTH - 48, 3 * DEPTH), jnp.bfloat16)], axis=0)

    def tags(block):
        pad = jnp.full((N, DEPTH - 3 * N), -1, jnp.int32)
        return jnp.concatenate([block.T, pad], axis=1)

    def coefficients(xs, y0, ny):
        lanes = lax.broadcasted_iota(jnp.int32, (ny, DEPTH), 1)
        slot = jnp.where(lanes < 48, lanes & 15, -9)
        at = pl.ds(y0, ny)
        tag = lt[at, :]
        hits = []
        for x in xs:
            c = x + N - XO
            hit = jnp.broadcast_to(tag[:, c:c + 1], (ny, DEPTH)) == slot
            hits.append(jnp.where(hit, 1.0, 0.0))
        onehot = jnp.concatenate(hits, axis=0).astype(jnp.bfloat16)
        out = jnp.dot(onehot, table, preferred_element_type=jnp.float32)
        for n, x in enumerate(xs):
            part = out[n * ny:(n + 1) * ny]
            s_ref[x, at, :] = part[:, :DEPTH]
            w_ref[x, at, :] = part[:, DEPTH:2 * DEPTH]
            k_ref[x, at, :] = part[:, 2 * DEPTH:]

    own_x = list(range(XO, XO + N))
    load_l.wait()
    none = jnp.full((N, N), -1, jnp.int32)
    lt[...] = jnp.full((NYF, DEPTH), -1, jnp.int32)
    lt[pl.ds(20, N), :] = tags(jnp.concatenate([none, lb[1, pl.ds(N, N), :], none], axis=0))

    def vertical(weight, value):
        return weight * pltpu.roll(value, DEPTH - 1, 1) + pltpu.roll(weight * value, 1, 1)

    zero = jnp.zeros((N, DEPTH), jnp.float32)
    pb[0, pl.ds(4, N), :] = zero
    pb[N + 1, pl.ds(4, N), :] = zero
    s_ref[XO - 1, pl.ds(YO, N), :] = zero
    s_ref[XO + N, pl.ds(YO, N), :] = zero
    own = pl.ds(YO, N)
    for h, (a, n) in enumerate(halves):
        coefficients(own_x[a:a + n], 16, 40)
        load_p[h].wait()
        load_s[h].wait()
        pb[pl.ds(1 + a, n), 3, :] = zero[:n]
        pb[pl.ds(1 + a, n), 4 + N, :] = zero[:n]

        @pl.loop(2 * h, 2 * h + 2)
        def _(i):
            out = []
            for x in [8 * i + n for n in range(8)]:
                fx = x + XO
                s = s_ref[fx, own, :]
                sn = [s_ref[fx - 1, own, :], s_ref[fx + 1, own, :],
                      s_ref[fx, pl.ds(YO - 1, N), :], s_ref[fx, pl.ds(YO + 1, N), :]]
                p = pb[x + 1, pl.ds(4, N), :]
                pn = [pb[x, pl.ds(4, N), :], pb[x + 2, pl.ds(4, N), :],
                      pb[x + 1, pl.ds(3, N), :], pb[x + 1, pl.ds(5, N), :]]
                flow = (s + sn[0]) * (p - pn[0])
                for n in range(1, 4):
                    flow = flow + (s + sn[n]) * (p - pn[n])
                both = k_ref[fx, own, :] - 4.0 * s
                flow = flow + (both * p - vertical(w_ref[fx, own, :], p))
                out.append(sb[x] - flow)
            for n in range(8):
                rb[8 * i + n + XO, own, :] = out[n]

        if h == 0:
            pl.semaphore_wait(barrier, count)
            start([1], SIDES)
            start([0], DIRS)
        start([2 + h], ORDER)

    def outward(s, sn, p, pn):
        return (s + sn) * (p - pn) - s * p

    arrive([0, 1], XSIDES)
    lt[pl.ds(20, N), :] = tags(lb[1])
    coefficients([XO - 1, XO + N], 16, 40)
    for e, (f, g) in enumerate(((XO, XO - 1), (XO + N - 1, XO + N))):
        s, sn = s_ref[f, own, :], s_ref[g, own, :]
        p, pn = pb[f - XO + 1, pl.ds(4, N), :], hx[e]
        delta = outward(s, sn, p, pn)
        ax[e] = delta
        bx[e] = outward(sn, s, pn, p)
        rx[e] = rb[f, own, :] - delta
    start([4], YSIDES)

    arrive([0, 1], YSIDES)
    lt[pl.ds(0, 20), :] = tags(jnp.concatenate([none, lb[0, pl.ds(N, N), :], none], axis=0))[12:]
    lt[pl.ds(52, 20), :] = tags(jnp.concatenate([none, lb[2, pl.ds(N, N), :], none], axis=0))[:20]
    coefficients(own_x, 16, 8)
    coefficients(own_x, 48, 8)
    rows = pl.ds(XO, N)
    for e, (f, g) in enumerate(((YO, YO - 1), (YO + N - 1, YO + N))):
        s, sn = s_ref[rows, f, :], s_ref[rows, g, :]
        p, pn = pb[pl.ds(1, N), f - YO + 4, :], hy[e]
        delta = outward(s, sn, p, pn)
        ay[e] = delta
        by[e] = outward(sn, s, pn, p)
        cy[e] = rb[rows, f, :] - delta
    for ex in (0, 1):
        for ey in (0, 1):
            cc[2 * ex + ey] = (rx[ex, pl.ds((N - 1) * ey, 1), :]
                               - ay[ey, pl.ds((N - 1) * ex, 1), :])
    start([5], XSIDES)
    start([6], CORNERS)

    arrive([0], CORNERS)
    lt[pl.ds(0, 20), :] = tags(lb[0])[12:]
    lt[pl.ds(52, 20), :] = tags(lb[2])[:20]
    for part in (range(0, XO - 1), range(XO + N + 1, NXF)):
        coefficients(list(part), 0, NYF)
    coefficients([XO - 1, XO + N], 0, 24)
    coefficients([XO - 1, XO + N], 48, 24)
    coefficients(own_x, 0, 16)
    coefficients(own_x, 56, 16)

    for x in range(XO - 13, XO + N + 13):
        y0, ny = columns(13, x)
        at = pl.ds(y0, ny)
        s = s_ref[x, at, :]
        diag = (k_ref[x, at, :] + (s_ref[x - 4, at, :] + s_ref[x + 4, at, :])
                + (s_ref[x, pl.ds(y0 - 4, ny), :] + s_ref[x, pl.ds(y0 + 4, ny), :]))
        k_ref[x, at, :] = jnp.where(s > 0.0, 0.8 / diag, 0.0)

    sent(list(KINDS), DIRS)
    for e, (f, g) in enumerate(((XO, XO - 1), (XO + N - 1, XO + N))):
        rb[f, own, :] = rb[f, own, :] - ax[e]
    for e, (f, g) in enumerate(((YO, YO - 1), (YO + N - 1, YO + N))):
        rb[rows, f, :] = rb[rows, f, :] - ay[e]
    arrive([2, 3, 4, 5, 6], ORDER)
    for e, g in enumerate((XO - 1, XO + N)):
        @pl.when(there(XSIDES[e]))
        def _():
            rb[g, own, :] = rb[g, own, :] - bx[e]
    for e, g in enumerate((YO - 1, YO + N)):
        @pl.when(there(YSIDES[e]))
        def _():
            rb[rows, g, :] = rb[rows, g, :] - by[e]


def relax(s_ref, w_ref, k_ref, rb, res_hbm, cor_hbm, ua, pa, ub, qb, uc, ob, local):
    out_r = pltpu.make_async_copy(rb.at[pl.ds(XO, N), pl.ds(YO, N), :], res_hbm, local.at[0])
    out_r.start()

    def vertical(weight, value):
        return weight * pltpu.roll(value, DEPTH - 1, 1) + pltpu.roll(weight * value, 1, 1)

    for x in range(XO - 13, XO + N + 13):
        y0, ny = columns(13, x)
        at = pl.ds(y0, ny)
        mean = (0.5 * rb[x, at, :]
                + 0.125 * (rb[x - 1, at, :] + rb[x + 1, at, :]
                           + rb[x, pl.ds(y0 - 1, ny), :] + rb[x, pl.ds(y0 + 1, ny), :]))
        u = k_ref[x, at, :] * mean
        ua[x, at, :] = u
        pa[x, at, :] = s_ref[x, at, :] * u

    def sweep(reach, u_in, p_in, u_out, p_out, base):
        for x in range(XO - reach, XO + N + reach):
            y0, ny = columns(reach, x)
            at = pl.ds(y0, ny)
            s = s_ref[x, at, :]
            u = u_in[x, at, :]
            un = (u_in[x - 4, at, :] + u_in[x + 4, at, :]
                  + u_in[x, pl.ds(y0 - 4, ny), :] + u_in[x, pl.ds(y0 + 4, ny), :])
            pn = (p_in[x - 4, at, :] + p_in[x + 4, at, :]
                  + p_in[x, pl.ds(y0 - 4, ny), :] + p_in[x, pl.ds(y0 + 4, ny), :])
            total = s * un + pn + vertical(w_ref[x, at, :], u)
            new = base[x, at, :] + 0.2 * u + k_ref[x, at, :] * total
            u_out[x, at, :] = new
            if p_out is not None:
                p_out[x, at, :] = s * new

    sweep(9, ua, pa, ub, qb, ua)
    sweep(5, ub, qb, uc, pa, ua)
    sweep(1, uc, pa, ub, None, ua)

    def out_c(c):
        rows = pl.ds(8 * c, 8)
        return pltpu.make_async_copy(ob.at[rows], cor_hbm.at[rows], local.at[1 + c])

    for c in range(4):
        @pl.loop(8 * c, 8 * c + 8, unroll=True)
        def _(x):
            fx = x + XO
            at = pl.ds(YO, N)
            ob[x] = (0.5 * ub[fx, at, :]
                     + 0.125 * (ub[fx - 1, at, :] + ub[fx + 1, at, :]
                                + ub[fx, pl.ds(YO - 1, N), :] + ub[fx, pl.ds(YO + 1, N), :]))

        out_c(c).start()
    out_r.wait()
    for c in range(4):
        out_c(c).wait()


def per_device(pressure, source, labels, region_table):
    hbm = pl.BlockSpec(memory_space=pltpu.HBM)
    vmem = pl.BlockSpec(memory_space=pltpu.VMEM)
    own = jax.ShapeDtypeStruct((N, N, DEPTH), jnp.float32)
    field = pltpu.VMEM((NXF, NYF, DEPTH), jnp.float32)
    fields = pl.pallas_call(
        exchange,
        out_shape=(field,) * 4,
        in_specs=[hbm] * 4,
        out_specs=(vmem,) * 4,
        scratch_shapes=[
            pltpu.VMEM((N + 2, 40, DEPTH), jnp.float32),
            pltpu.VMEM((N, N, DEPTH), jnp.float32),
            pltpu.VMEM((16, DEPTH), jnp.float32),
            pltpu.VMEM((3, 3 * N, N), jnp.int32),
            pltpu.VMEM((NYF, DEPTH), jnp.int32),
        ] + [pltpu.VMEM((2, N, DEPTH), jnp.float32)] * 8 + [
            pltpu.VMEM((4, 1, DEPTH), jnp.float32),
            pltpu.SemaphoreType.DMA((len(KEYS),)),
            pltpu.SemaphoreType.DMA((len(KEYS),)),
            pltpu.SemaphoreType.DMA((6,)),
        ],
        compiler_params=pltpu.CompilerParams(
            collective_id=0, has_side_effects=True, vmem_limit_bytes=24 << 20),
        name="exchange",
    )(*[pltpu.with_memory_space_constraint(a, pltpu.HBM)
        for a in (pressure, source, labels, region_table)])
    return pl.pallas_call(
        relax,
        out_shape=(own, own),
        in_specs=[vmem] * 4,
        out_specs=(hbm, hbm),
        scratch_shapes=[field] * 5 + [
            pltpu.VMEM((N, N, DEPTH), jnp.float32),
            pltpu.SemaphoreType.DMA((5,)),
        ],
        compiler_params=pltpu.CompilerParams(vmem_limit_bytes=24 << 20),
        name="relax",
    )(*fields)


def solution(mesh):
    placed = (P("space", "group", None), P("space", "group", None), P("space", "group"), P())
    return jax.shard_map(
        per_device,
        mesh=mesh,
        in_specs=placed,
        out_specs=(P("space", "group", None), P("space", "group", None)),
        check_vma=False,
    )
```

```python
import jax
import jax.numpy as jnp
from jax import lax
from jax.experimental import pallas as pl
from jax.experimental.pallas import tpu as pltpu
from jax.sharding import PartitionSpec as P

MESH = pl.DeviceIdType.MESH
N = 32
DEPTH = 128
XO, YO = 17, 20
NXF, NYF = 66, 72
DIRS = [(dx, dy) for dx in (-1, 0, 1) for dy in (-1, 0, 1) if (dx, dy) != (0, 0)]
ORDER = [(0, -1), (0, 1), (-1, -1), (-1, 1), (1, -1), (1, 1), (-1, 0), (1, 0)]
DIRS_X, DIRS_Y = [(-1, 0), (1, 0)], [(0, -1), (0, 1)]
DIRS_XY = [(-1, -1), (-1, 1), (1, -1), (1, 1)]
SIDES = DIRS_X + DIRS_Y


def pieces(d, stage):
    dx, dy = d
    if dy == 0:
        return [((1, 14), (1, N - 2))] if stage == (dx > 0) else []
    if dx == 0:
        return [((1, 15), (1, 14)) if stage == 0 else ((16, N - 2), (1, 14))]
    return [((2, 6), (2, 12)), ((7, 12), (2, 6))] if stage == (dx > 0) else []


def span(step, lo, hi):
    if step == 1:
        return N - hi, hi - lo + 1
    if step == -1:
        return lo - 1, hi - lo + 1
    return lo, hi - lo + 1


XSIDES, YSIDES, CORNERS = DIRS_X, DIRS_Y, DIRS_XY
KINDS = {0: DIRS, 1: SIDES, 2: DIRS, 3: DIRS, 4: YSIDES, 5: XSIDES, 6: CORNERS}
KEYS = [(kind, d, n) for kind, dirs in KINDS.items() for d in dirs
        for n in range(len(pieces(d, kind - 2)) if kind in (2, 3) else (1, 1, 0, 0, 2, 2, 3)[kind])]


def columns(reach, x):
    beyond = max(XO - x, x - (XO + N - 1), 1)
    side = reach - 4 * (-(-(beyond - 1) // 4))
    return YO - side - 3, -(-(N + 2 * side) // 8) * 8


def exchange(p_hbm, src_hbm, lab_hbm, tab_hbm, s_ref, w_ref, k_ref, rb,
             pb, sb, tb, lbl, pk, lpk, lt, hx, hy, ax, ay, bx, by, rx, cy, cc,
             send, recv, local):
    groups = lax.axis_size("group")
    spaces = lax.axis_size("space")
    gi = lax.axis_index("group")
    si = lax.axis_index("space")

    def there(d):
        dx, dy = d
        ok = None
        if dx == 1:
            ok = si < spaces - 1
        elif dx == -1:
            ok = si > 0
        if dy:
            okg = gi < groups - 1 if dy == 1 else gi > 0
            ok = okg if ok is None else jnp.logical_and(ok, okg)
        return ok

    def back(d):
        return (-d[0], -d[1])

    def device(d):
        return (gi + d[1], si + d[0])

    halves = ((0, 17), (17, 15))
    load_p = [pltpu.make_async_copy(p_hbm.at[pl.ds(a, n)], pb.at[pl.ds(1 + a, n), pl.ds(4, N), :],
                                    local.at[4 + h]) for h, (a, n) in enumerate(halves)]
    load_s = [pltpu.make_async_copy(src_hbm.at[pl.ds(a, n)], sb.at[pl.ds(a, n)],
                                    local.at[h]) for h, (a, n) in enumerate(halves)]
    load_l = pltpu.make_async_copy(lab_hbm, lbl, local.at[2])
    load_t = pltpu.make_async_copy(tab_hbm, tb, local.at[3])
    load_l.start()
    load_t.start()
    for h in (0, 1):
        load_p[h].start()
        load_s[h].start()

    barrier = pltpu.get_barrier_semaphore()
    count = jnp.int32(0)
    for d in DIRS:
        ok = there(d)
        count = count + ok.astype(jnp.int32)

        @pl.when(ok)
        def _():
            pl.semaphore_signal(barrier, 1, device_id=device(d), device_id_type=MESH)

    for d in DIRS:
        @pl.when(jnp.logical_not(there(d)))
        def _():
            dx, dy = d
            lpk[1 + dy, 1 + dx] = jnp.full((8, DEPTH), -1, jnp.int32)

    for d in SIDES:
        @pl.when(jnp.logical_not(there(d)))
        def _():
            dx, dy = d
            if dx:
                hx[int(dx > 0)] = jnp.zeros((N, DEPTH), jnp.float32)
                r0 = XO - 14 if dx < 0 else XO + N

                @pl.loop(0, 14)
                def _(i):
                    rb[r0 + i] = jnp.zeros((NYF, DEPTH), jnp.float32)
            else:
                hy[int(dy > 0)] = jnp.zeros((N, DEPTH), jnp.float32)
                c0 = YO - 14 if dy < 0 else YO + N

                @pl.loop(XO - 14, XO + N + 14)
                def _(i):
                    rb[i, pl.ds(c0, 14), :] = jnp.zeros((14, DEPTH), jnp.float32)

    def messages(kind, d):
        dx, dy = d
        ex, ey = int(dx > 0), int(dy > 0)
        last = N - 1
        if kind == 0:
            ends = [(pk, lpk.at[1 - dy, 1 - dx])]
        elif kind == 1:
            ends = [(p_hbm.at[last * ex], hx.at[1 - ex]) if dx
                    else (p_hbm.at[:, last * ey, :], hy.at[1 - ey])]
        elif kind in (2, 3):
            ends = []
            for rows, cols in pieces(d, kind - 2):
                x, nx = span(dx, *rows)
                y, ny = span(dy, *cols)
                x = x + XO
                y = y + YO
                ends.append((rb.at[pl.ds(x, nx), pl.ds(y, ny), :],
                             rb.at[pl.ds(x - N * dx, nx), pl.ds(y - N * dy, ny), :]))
        elif kind == 4:
            y = (N - 14) * ey
            ends = [(rx.at[e, pl.ds(y, 14), :],
                     rb.at[XO + last * e, pl.ds(YO + y - N * dy, 14), :]) for e in (0, 1)]
        elif kind == 5:
            x = (N - 14) * ex
            ends = [(cy.at[e, pl.ds(x, 14), :],
                     rb.at[pl.ds(XO + x - N * dx, 14), YO + last * e, :]) for e in (0, 1)]
        else:
            x, y = (N - 13 if ex else 1), (N - 13 if ey else 1)
            fx, fy = XO + last * ex - N * dx, YO + last * ey - N * dy
            ends = [(rx.at[ex, pl.ds(y, 12), :], rb.at[fx, pl.ds(YO + y - N * dy, 12), :]),
                    (cy.at[ey, pl.ds(x, 12), :], rb.at[pl.ds(XO + x - N * dx, 12), fy, :]),
                    (cc.at[2 * ex + ey], rb.at[fx, pl.ds(fy, 1), :])]
        return [pltpu.make_async_remote_copy(
            src_ref=src, dst_ref=dst, send_sem=send.at[KEYS.index((kind, d, n))],
            recv_sem=recv.at[KEYS.index((kind, d, n))], device_id=device(d), device_id_type=MESH)
            for n, (src, dst) in enumerate(ends)]

    def held(kinds, d):
        return [k for k in kinds if any(key[:2] == (k, d) for key in KEYS)]

    def start(kinds, dirs):
        for d in dirs:
            if not held(kinds, d):
                continue

            @pl.when(there(d))
            def _():
                for kind in held(kinds, d):
                    for m in messages(kind, d):
                        m.start()

    def arrive(kinds, dirs):
        for d in dirs:
            @pl.when(there(back(d)))
            def _():
                for kind in held(kinds, d):
                    for m in messages(kind, d):
                        m.wait_recv()

    def sent(kinds, dirs):
        for d in dirs:
            @pl.when(there(d))
            def _():
                for kind in held(kinds, d):
                    for m in messages(kind, d):
                        m.wait_send()


    load_t.wait()
    half = 0.5 * tb[...]
    lane = lax.broadcasted_iota(jnp.int32, (16, DEPTH), 1)
    up = jnp.where(lane < DEPTH - 1, pltpu.roll(half, DEPTH - 1, 1), 0.0)
    down = jnp.where(lane > 0, pltpu.roll(half, 1, 1), 0.0)
    wup = jnp.where(lane < DEPTH - 1, half + up, 0.0)
    vert = 6.0 * half + (up + down)
    wide = jnp.concatenate([half, wup, vert], axis=1)
    hi = wide.astype(jnp.bfloat16)
    rest = wide - hi.astype(jnp.float32)
    mid = rest.astype(jnp.bfloat16)
    low = (rest - mid.astype(jnp.float32)).astype(jnp.bfloat16)
    table = jnp.concatenate(
        [hi, mid, low, jnp.zeros((DEPTH - 48, 3 * DEPTH), jnp.bfloat16)], axis=0)

    def tags(block):
        pad = jnp.full((N, DEPTH - 3 * N), -1, jnp.int32)
        return jnp.concatenate([block.T, pad], axis=1)

    def coefficients(xs, y0, ny):
        lanes = lax.broadcasted_iota(jnp.int32, (ny, DEPTH), 1)
        slot = jnp.where(lanes < 48, lanes & 15, -9)
        at = pl.ds(y0, ny)
        tag = lt[at, :]
        hits = []
        for x in xs:
            c = x + N - XO
            hit = jnp.broadcast_to(tag[:, c:c + 1], (ny, DEPTH)) == slot
            hits.append(jnp.where(hit, 1.0, 0.0))
        onehot = jnp.concatenate(hits, axis=0).astype(jnp.bfloat16)
        out = jnp.dot(onehot, table, preferred_element_type=jnp.float32)
        for n, x in enumerate(xs):
            part = out[n * ny:(n + 1) * ny]
            s_ref[x, at, :] = part[:, :DEPTH]
            w_ref[x, at, :] = part[:, DEPTH:2 * DEPTH]
            k_ref[x, at, :] = part[:, 2 * DEPTH:]

    own_x = list(range(XO, XO + N))
    load_l.wait()
    none = jnp.full((N, N), -1, jnp.int32)
    mine = lbl[...]
    pk[...] = jnp.concatenate([mine[8 * g:8 * g + 8] for g in range(4)], axis=1)

    def block(dy, dx):
        tile = lpk[dy, dx]
        return jnp.concatenate([tile[:, N * g:N * g + N] for g in range(4)], axis=0)

    lt[...] = jnp.full((NYF, DEPTH), -1, jnp.int32)
    lt[pl.ds(20, N), :] = tags(jnp.concatenate([none, mine, none], axis=0))

    def vertical(weight, value):
        return weight * pltpu.roll(value, DEPTH - 1, 1) + pltpu.roll(weight * value, 1, 1)

    zero = jnp.zeros((N, DEPTH), jnp.float32)
    pb[0, pl.ds(4, N), :] = zero
    pb[N + 1, pl.ds(4, N), :] = zero
    s_ref[XO - 1, pl.ds(YO, N), :] = zero
    s_ref[XO + N, pl.ds(YO, N), :] = zero
    own = pl.ds(YO, N)
    for h, (a, n) in enumerate(halves):
        coefficients(own_x[a:a + n], 16, 40)
        load_p[h].wait()
        load_s[h].wait()
        pb[pl.ds(1 + a, n), 3, :] = zero[:n]
        pb[pl.ds(1 + a, n), 4 + N, :] = zero[:n]

        @pl.loop(2 * h, 2 * h + 2)
        def _(i):
            out = []
            for x in [8 * i + n for n in range(8)]:
                fx = x + XO
                s = s_ref[fx, own, :]
                sn = [s_ref[fx - 1, own, :], s_ref[fx + 1, own, :],
                      s_ref[fx, pl.ds(YO - 1, N), :], s_ref[fx, pl.ds(YO + 1, N), :]]
                p = pb[x + 1, pl.ds(4, N), :]
                pn = [pb[x, pl.ds(4, N), :], pb[x + 2, pl.ds(4, N), :],
                      pb[x + 1, pl.ds(3, N), :], pb[x + 1, pl.ds(5, N), :]]
                flow = (s + sn[0]) * (p - pn[0])
                for n in range(1, 4):
                    flow = flow + (s + sn[n]) * (p - pn[n])
                both = k_ref[fx, own, :] - 4.0 * s
                flow = flow + (both * p - vertical(w_ref[fx, own, :], p))
                out.append(sb[x] - flow)
            for n in range(8):
                rb[8 * i + n + XO, own, :] = out[n]

        if h == 0:
            pl.semaphore_wait(barrier, count)
            start([0], ORDER)
            start([1], SIDES)
        start([2 + h], ORDER)

    def outward(s, sn, p, pn):
        return (s + sn) * (p - pn) - s * p

    arrive([0, 1], XSIDES)
    lt[pl.ds(20, N), :] = tags(jnp.concatenate([block(1, 0), mine, block(1, 2)], axis=0))
    coefficients([XO - 1, XO + N], 16, 40)
    for e, (f, g) in enumerate(((XO, XO - 1), (XO + N - 1, XO + N))):
        s, sn = s_ref[f, own, :], s_ref[g, own, :]
        p, pn = pb[f - XO + 1, pl.ds(4, N), :], hx[e]
        delta = outward(s, sn, p, pn)
        ax[e] = delta
        bx[e] = outward(sn, s, pn, p)
        rx[e] = rb[f, own, :] - delta
    start([4], YSIDES)

    arrive([0, 1], YSIDES)
    lt[pl.ds(0, 20), :] = tags(jnp.concatenate([none, block(0, 1), none], axis=0))[12:]
    lt[pl.ds(52, 20), :] = tags(jnp.concatenate([none, block(2, 1), none], axis=0))[:20]
    coefficients(own_x, 16, 8)
    coefficients(own_x, 48, 8)
    rows = pl.ds(XO, N)
    for e, (f, g) in enumerate(((YO, YO - 1), (YO + N - 1, YO + N))):
        s, sn = s_ref[rows, f, :], s_ref[rows, g, :]
        p, pn = pb[pl.ds(1, N), f - YO + 4, :], hy[e]
        delta = outward(s, sn, p, pn)
        ay[e] = delta
        by[e] = outward(sn, s, pn, p)
        cy[e] = rb[rows, f, :] - delta
    for ex in (0, 1):
        for ey in (0, 1):
            cc[2 * ex + ey] = (rx[ex, pl.ds((N - 1) * ey, 1), :]
                               - ay[ey, pl.ds((N - 1) * ex, 1), :])
    start([5], XSIDES)
    start([6], CORNERS)

    arrive([0], CORNERS)
    lt[pl.ds(0, 20), :] = tags(jnp.concatenate([block(0, n) for n in range(3)], axis=0))[12:]
    lt[pl.ds(52, 20), :] = tags(jnp.concatenate([block(2, n) for n in range(3)], axis=0))[:20]
    for part in (range(0, XO - 1), range(XO + N + 1, NXF)):
        coefficients(list(part), 0, NYF)
    coefficients([XO - 1, XO + N], 0, 24)
    coefficients([XO - 1, XO + N], 48, 24)
    coefficients(own_x, 0, 16)
    coefficients(own_x, 56, 16)

    for x in range(XO - 13, XO + N + 13):
        y0, ny = columns(13, x)
        at = pl.ds(y0, ny)
        s = s_ref[x, at, :]
        diag = (k_ref[x, at, :] + (s_ref[x - 4, at, :] + s_ref[x + 4, at, :])
                + (s_ref[x, pl.ds(y0 - 4, ny), :] + s_ref[x, pl.ds(y0 + 4, ny), :]))
        k_ref[x, at, :] = jnp.where(s > 0.0, 0.8 / diag, 0.0)

    sent(list(KINDS), DIRS)
    for e, (f, g) in enumerate(((XO, XO - 1), (XO + N - 1, XO + N))):
        rb[f, own, :] = rb[f, own, :] - ax[e]
    for e, (f, g) in enumerate(((YO, YO - 1), (YO + N - 1, YO + N))):
        rb[rows, f, :] = rb[rows, f, :] - ay[e]
    arrive([2, 3, 4, 5, 6], ORDER)
    for e, g in enumerate((XO - 1, XO + N)):
        @pl.when(there(XSIDES[e]))
        def _():
            rb[g, own, :] = rb[g, own, :] - bx[e]
    for e, g in enumerate((YO - 1, YO + N)):
        @pl.when(there(YSIDES[e]))
        def _():
            rb[rows, g, :] = rb[rows, g, :] - by[e]


def relax(s_ref, w_ref, k_ref, rb, res_hbm, cor_hbm, ua, pa, ub, qb, uc, ob, local):
    out_r = pltpu.make_async_copy(rb.at[pl.ds(XO, N), pl.ds(YO, N), :], res_hbm, local.at[0])
    out_r.start()

    def vertical(weight, value):
        return weight * pltpu.roll(value, DEPTH - 1, 1) + pltpu.roll(weight * value, 1, 1)

    for x in range(XO - 13, XO + N + 13):
        y0, ny = columns(13, x)
        at = pl.ds(y0, ny)
        mean = (0.5 * rb[x, at, :]
                + 0.125 * (rb[x - 1, at, :] + rb[x + 1, at, :]
                           + rb[x, pl.ds(y0 - 1, ny), :] + rb[x, pl.ds(y0 + 1, ny), :]))
        u = k_ref[x, at, :] * mean
        ua[x, at, :] = u
        pa[x, at, :] = s_ref[x, at, :] * u

    def sweep(reach, u_in, p_in, u_out, p_out, base):
        for x in range(XO - reach, XO + N + reach):
            y0, ny = columns(reach, x)
            at = pl.ds(y0, ny)
            s = s_ref[x, at, :]
            u = u_in[x, at, :]
            un = (u_in[x - 4, at, :] + u_in[x + 4, at, :]
                  + u_in[x, pl.ds(y0 - 4, ny), :] + u_in[x, pl.ds(y0 + 4, ny), :])
            pn = (p_in[x - 4, at, :] + p_in[x + 4, at, :]
                  + p_in[x, pl.ds(y0 - 4, ny), :] + p_in[x, pl.ds(y0 + 4, ny), :])
            total = s * un + pn + vertical(w_ref[x, at, :], u)
            new = base[x, at, :] + 0.2 * u + k_ref[x, at, :] * total
            u_out[x, at, :] = new
            if p_out is not None:
                p_out[x, at, :] = s * new

    sweep(9, ua, pa, ub, qb, ua)
    sweep(5, ub, qb, uc, pa, ua)
    sweep(1, uc, pa, ub, None, ua)

    def out_c(c):
        rows = pl.ds(8 * c, 8)
        return pltpu.make_async_copy(ob.at[rows], cor_hbm.at[rows], local.at[1 + c])

    for c in range(4):
        @pl.loop(8 * c, 8 * c + 8, unroll=True)
        def _(x):
            fx = x + XO
            at = pl.ds(YO, N)
            ob[x] = (0.5 * ub[fx, at, :]
                     + 0.125 * (ub[fx - 1, at, :] + ub[fx + 1, at, :]
                                + ub[fx, pl.ds(YO - 1, N), :] + ub[fx, pl.ds(YO + 1, N), :]))

        out_c(c).start()
    out_r.wait()
    for c in range(4):
        out_c(c).wait()


def per_device(pressure, source, labels, region_table):
    hbm = pl.BlockSpec(memory_space=pltpu.HBM)
    vmem = pl.BlockSpec(memory_space=pltpu.VMEM)
    own = jax.ShapeDtypeStruct((N, N, DEPTH), jnp.float32)
    field = pltpu.VMEM((NXF, NYF, DEPTH), jnp.float32)
    fields = pl.pallas_call(
        exchange,
        out_shape=(field,) * 4,
        in_specs=[hbm] * 4,
        out_specs=(vmem,) * 4,
        scratch_shapes=[
            pltpu.VMEM((N + 2, 40, DEPTH), jnp.float32),
            pltpu.VMEM((N, N, DEPTH), jnp.float32),
            pltpu.VMEM((16, DEPTH), jnp.float32),
            pltpu.VMEM((N, N), jnp.int32),
            pltpu.VMEM((8, DEPTH), jnp.int32),
            pltpu.VMEM((3, 3, 8, DEPTH), jnp.int32),
            pltpu.VMEM((NYF, DEPTH), jnp.int32),
        ] + [pltpu.VMEM((2, N, DEPTH), jnp.float32)] * 8 + [
            pltpu.VMEM((4, 1, DEPTH), jnp.float32),
            pltpu.SemaphoreType.DMA((len(KEYS),)),
            pltpu.SemaphoreType.DMA((len(KEYS),)),
            pltpu.SemaphoreType.DMA((6,)),
        ],
        compiler_params=pltpu.CompilerParams(
            collective_id=0, has_side_effects=True, vmem_limit_bytes=24 << 20),
        name="exchange",
    )(*[pltpu.with_memory_space_constraint(a, pltpu.HBM)
        for a in (pressure, source, labels, region_table)])
    return pl.pallas_call(
        relax,
        out_shape=(own, own),
        in_specs=[vmem] * 4,
        out_specs=(hbm, hbm),
        scratch_shapes=[field] * 5 + [
            pltpu.VMEM((N, N, DEPTH), jnp.float32),
            pltpu.SemaphoreType.DMA((5,)),
        ],
        compiler_params=pltpu.CompilerParams(vmem_limit_bytes=24 << 20),
        name="relax",
    )(*fields)


def solution(mesh):
    placed = (P("space", "group", None), P("space", "group", None), P("space", "group"), P())
    return jax.shard_map(
        per_device,
        mesh=mesh,
        in_specs=placed,
        out_specs=(P("space", "group", None), P("space", "group", None)),
        check_vma=False,
    )
```

```python
import jax
import jax.numpy as jnp
from jax import lax
from jax.experimental import pallas as pl
from jax.experimental.pallas import tpu as pltpu
from jax.sharding import PartitionSpec as P

MESH = pl.DeviceIdType.MESH
N = 32
DEPTH = 128
XO, YO = 17, 20
NXF, NYF = 66, 72
DIRS = [(dx, dy) for dx in (-1, 0, 1) for dy in (-1, 0, 1) if (dx, dy) != (0, 0)]
ORDER = [(0, -1), (0, 1), (-1, 0), (1, 0), (-1, -1), (-1, 1), (1, -1), (1, 1)]
DIRS_X, DIRS_Y = [(-1, 0), (1, 0)], [(0, -1), (0, 1)]
DIRS_XY = [(-1, -1), (-1, 1), (1, -1), (1, 1)]
SIDES = DIRS_X + DIRS_Y


def pieces(d, stage):
    dx, dy = d
    if dy == 0:
        return [((1, 14), (1, N - 2))] if stage == (dx > 0) else []
    if dx == 0:
        return [((1, 15), (1, 14)) if stage == 0 else ((16, N - 2), (1, 14))]
    return [((2, 6), (2, 12)), ((7, 12), (2, 6))] if stage == (dx > 0) else []


def span(step, lo, hi):
    if step == 1:
        return N - hi, hi - lo + 1
    if step == -1:
        return lo - 1, hi - lo + 1
    return lo, hi - lo + 1


XSIDES, YSIDES, CORNERS = DIRS_X, DIRS_Y, DIRS_XY
KINDS = {0: DIRS, 1: SIDES, 2: DIRS, 3: DIRS, 4: YSIDES, 5: XSIDES, 6: CORNERS}
KEYS = [(kind, d, n) for kind, dirs in KINDS.items() for d in dirs
        for n in range(len(pieces(d, kind - 2)) if kind in (2, 3) else (1, 1, 0, 0, 2, 2, 2)[kind])]


def columns(reach, x):
    beyond = max(XO - x, x - (XO + N - 1), 1)
    side = reach - 4 * (-(-(beyond - 1) // 4))
    return YO - side - 3, -(-(N + 2 * side) // 8) * 8


def exchange(p_hbm, src_hbm, lab_hbm, tab_hbm, s_ref, w_ref, k_ref, rb,
             pb, sb, tb, lbl, pk, lpk, lt, hx, hy, ax, ay, bx, by, rx, cy, rc,
             send, recv, local):
    groups = lax.axis_size("group")
    spaces = lax.axis_size("space")
    gi = lax.axis_index("group")
    si = lax.axis_index("space")

    def there(d):
        dx, dy = d
        ok = None
        if dx == 1:
            ok = si < spaces - 1
        elif dx == -1:
            ok = si > 0
        if dy:
            okg = gi < groups - 1 if dy == 1 else gi > 0
            ok = okg if ok is None else jnp.logical_and(ok, okg)
        return ok

    def back(d):
        return (-d[0], -d[1])

    def device(d):
        return (gi + d[1], si + d[0])

    halves = ((0, 17), (17, 15))
    load_p = [pltpu.make_async_copy(p_hbm.at[pl.ds(a, n)], pb.at[pl.ds(1 + a, n), pl.ds(4, N), :],
                                    local.at[4 + h]) for h, (a, n) in enumerate(halves)]
    load_s = [pltpu.make_async_copy(src_hbm.at[pl.ds(a, n)], sb.at[pl.ds(a, n)],
                                    local.at[h]) for h, (a, n) in enumerate(halves)]
    load_l = pltpu.make_async_copy(lab_hbm, lbl, local.at[2])
    load_t = pltpu.make_async_copy(tab_hbm, tb, local.at[3])
    load_l.start()
    load_t.start()
    for h in (0, 1):
        load_p[h].start()
        load_s[h].start()

    barrier = pltpu.get_barrier_semaphore()
    count = jnp.int32(0)
    for d in DIRS:
        ok = there(d)
        count = count + ok.astype(jnp.int32)

        @pl.when(ok)
        def _():
            pl.semaphore_signal(barrier, 1, device_id=device(d), device_id_type=MESH)

    for d in DIRS:
        @pl.when(jnp.logical_not(there(d)))
        def _():
            dx, dy = d
            lpk[1 + dy, 1 + dx] = jnp.full((8, DEPTH), -1, jnp.int32)

    for d in SIDES:
        @pl.when(jnp.logical_not(there(d)))
        def _():
            dx, dy = d
            if dx:
                hx[int(dx > 0)] = jnp.zeros((N, DEPTH), jnp.float32)
                r0 = XO - 14 if dx < 0 else XO + N

                @pl.loop(0, 14)
                def _(i):
                    rb[r0 + i] = jnp.zeros((NYF, DEPTH), jnp.float32)
            else:
                hy[int(dy > 0)] = jnp.zeros((N, DEPTH), jnp.float32)
                c0 = YO - 14 if dy < 0 else YO + N

                @pl.loop(XO - 14, XO + N + 14)
                def _(i):
                    rb[i, pl.ds(c0, 14), :] = jnp.zeros((14, DEPTH), jnp.float32)

    def messages(kind, d):
        dx, dy = d
        ex, ey = int(dx > 0), int(dy > 0)
        last = N - 1
        if kind == 0:
            ends = [(pk, lpk.at[1 - dy, 1 - dx])]
        elif kind == 1:
            ends = [(p_hbm.at[last * ex], hx.at[1 - ex]) if dx
                    else (p_hbm.at[:, last * ey, :], hy.at[1 - ey])]
        elif kind in (2, 3):
            ends = []
            for rows, cols in pieces(d, kind - 2):
                x, nx = span(dx, *rows)
                y, ny = span(dy, *cols)
                x = x + XO
                y = y + YO
                ends.append((rb.at[pl.ds(x, nx), pl.ds(y, ny), :],
                             rb.at[pl.ds(x - N * dx, nx), pl.ds(y - N * dy, ny), :]))
        elif kind == 4:
            y = (N - 14) * ey
            ends = [(rx.at[e, pl.ds(y, 14), :],
                     rb.at[XO + last * e, pl.ds(YO + y - N * dy, 14), :]) for e in (0, 1)]
        elif kind == 5:
            x = (N - 14) * ex
            ends = [(cy.at[e, pl.ds(x, 14), :],
                     rb.at[pl.ds(XO + x - N * dx, 14), YO + last * e, :]) for e in (0, 1)]
        else:
            x, y = (N - 13 if ex else 1), (N - 13) * ey
            fx, fy = XO + last * ex - N * dx, YO + last * ey - N * dy
            ends = [(rc.at[ex, pl.ds(y, 13), :], rb.at[fx, pl.ds(YO + y - N * dy, 13), :]),
                    (cy.at[ey, pl.ds(x, 12), :], rb.at[pl.ds(XO + x - N * dx, 12), fy, :])]
        return [pltpu.make_async_remote_copy(
            src_ref=src, dst_ref=dst, send_sem=send.at[KEYS.index((kind, d, n))],
            recv_sem=recv.at[KEYS.index((kind, d, n))], device_id=device(d), device_id_type=MESH)
            for n, (src, dst) in enumerate(ends)]

    def held(kinds, d):
        return [k for k in kinds if any(key[:2] == (k, d) for key in KEYS)]

    def start(kinds, dirs):
        for d in dirs:
            if not held(kinds, d):
                continue

            @pl.when(there(d))
            def _():
                for kind in held(kinds, d):
                    for m in messages(kind, d):
                        m.start()

    def arrive(kinds, dirs):
        for d in dirs:
            @pl.when(there(back(d)))
            def _():
                for kind in held(kinds, d):
                    for m in messages(kind, d):
                        m.wait_recv()

    def sent(kinds, dirs):
        for d in dirs:
            @pl.when(there(d))
            def _():
                for kind in held(kinds, d):
                    for m in messages(kind, d):
                        m.wait_send()


    load_t.wait()
    half = 0.5 * tb[...]
    lane = lax.broadcasted_iota(jnp.int32, (16, DEPTH), 1)
    up = jnp.where(lane < DEPTH - 1, pltpu.roll(half, DEPTH - 1, 1), 0.0)
    down = jnp.where(lane > 0, pltpu.roll(half, 1, 1), 0.0)
    wup = jnp.where(lane < DEPTH - 1, half + up, 0.0)
    vert = 6.0 * half + (up + down)
    wide = jnp.concatenate([half, wup, vert], axis=1)
    hi = wide.astype(jnp.bfloat16)
    rest = wide - hi.astype(jnp.float32)
    mid = rest.astype(jnp.bfloat16)
    low = (rest - mid.astype(jnp.float32)).astype(jnp.bfloat16)
    table = jnp.concatenate(
        [hi, mid, low, jnp.zeros((DEPTH - 48, 3 * DEPTH), jnp.bfloat16)], axis=0)

    def tags(block):
        pad = jnp.full((N, DEPTH - 3 * N), -1, jnp.int32)
        return jnp.concatenate([block.T, pad], axis=1)

    def coefficients(xs, y0, ny):
        lanes = lax.broadcasted_iota(jnp.int32, (ny, DEPTH), 1)
        slot = jnp.where(lanes < 48, lanes & 15, -9)
        at = pl.ds(y0, ny)
        tag = lt[at, :]
        hits = []
        for x in xs:
            c = x + N - XO
            hit = jnp.broadcast_to(tag[:, c:c + 1], (ny, DEPTH)) == slot
            hits.append(jnp.where(hit, 1.0, 0.0))
        onehot = jnp.concatenate(hits, axis=0).astype(jnp.bfloat16)
        out = jnp.dot(onehot, table, preferred_element_type=jnp.float32)
        for n, x in enumerate(xs):
            part = out[n * ny:(n + 1) * ny]
            s_ref[x, at, :] = part[:, :DEPTH]
            w_ref[x, at, :] = part[:, DEPTH:2 * DEPTH]
            k_ref[x, at, :] = part[:, 2 * DEPTH:]

    own_x = list(range(XO, XO + N))
    load_l.wait()
    none = jnp.full((N, N), -1, jnp.int32)
    mine = lbl[...]
    pk[...] = jnp.concatenate([mine[8 * g:8 * g + 8] for g in range(4)], axis=1)

    def block(dy, dx):
        tile = lpk[dy, dx]
        return jnp.concatenate([tile[:, N * g:N * g + N] for g in range(4)], axis=0)

    lt[...] = jnp.full((NYF, DEPTH), -1, jnp.int32)
    lt[pl.ds(20, N), :] = tags(jnp.concatenate([none, mine, none], axis=0))

    def vertical(weight, value):
        return weight * pltpu.roll(value, DEPTH - 1, 1) + pltpu.roll(weight * value, 1, 1)

    zero = jnp.zeros((N, DEPTH), jnp.float32)
    pb[0, pl.ds(4, N), :] = zero
    pb[N + 1, pl.ds(4, N), :] = zero
    s_ref[XO - 1, pl.ds(YO, N), :] = zero
    s_ref[XO + N, pl.ds(YO, N), :] = zero
    own = pl.ds(YO, N)
    for h, (a, n) in enumerate(halves):
        coefficients(own_x[a:a + n], 16, 40)
        load_p[h].wait()
        load_s[h].wait()
        pb[pl.ds(1 + a, n), 3, :] = zero[:n]
        pb[pl.ds(1 + a, n), 4 + N, :] = zero[:n]

        @pl.loop(2 * h, 2 * h + 2)
        def _(i):
            out = []
            for x in [8 * i + n for n in range(8)]:
                fx = x + XO
                s = s_ref[fx, own, :]
                sn = [s_ref[fx - 1, own, :], s_ref[fx + 1, own, :],
                      s_ref[fx, pl.ds(YO - 1, N), :], s_ref[fx, pl.ds(YO + 1, N), :]]
                p = pb[x + 1, pl.ds(4, N), :]
                pn = [pb[x, pl.ds(4, N), :], pb[x + 2, pl.ds(4, N), :],
                      pb[x + 1, pl.ds(3, N), :], pb[x + 1, pl.ds(5, N), :]]
                flow = (s + sn[0]) * (p - pn[0])
                for n in range(1, 4):
                    flow = flow + (s + sn[n]) * (p - pn[n])
                both = k_ref[fx, own, :] - 4.0 * s
                flow = flow + (both * p - vertical(w_ref[fx, own, :], p))
                out.append(sb[x] - flow)
            for n in range(8):
                rb[8 * i + n + XO, own, :] = out[n]

        if h == 0:
            pl.semaphore_wait(barrier, count)
            start([0], ORDER)
            start([1], SIDES)
        start([2 + h], ORDER)

    def outward(s, sn, p, pn):
        return (s + sn) * (p - pn) - s * p

    arrive([0, 1], XSIDES)
    lt[pl.ds(20, N), :] = tags(jnp.concatenate([block(1, 0), mine, block(1, 2)], axis=0))
    coefficients([XO - 1, XO + N], 16, 40)
    for e, (f, g) in enumerate(((XO, XO - 1), (XO + N - 1, XO + N))):
        s, sn = s_ref[f, own, :], s_ref[g, own, :]
        p, pn = pb[f - XO + 1, pl.ds(4, N), :], hx[e]
        delta = outward(s, sn, p, pn)
        ax[e] = delta
        bx[e] = outward(sn, s, pn, p)
        rx[e] = rb[f, own, :] - delta
    start([4], YSIDES)

    arrive([0, 1], YSIDES)
    lt[pl.ds(0, 20), :] = tags(jnp.concatenate([none, block(0, 1), none], axis=0))[12:]
    lt[pl.ds(52, 20), :] = tags(jnp.concatenate([none, block(2, 1), none], axis=0))[:20]
    coefficients(own_x, 16, 8)
    coefficients(own_x, 48, 8)
    rows = pl.ds(XO, N)
    for e, (f, g) in enumerate(((YO, YO - 1), (YO + N - 1, YO + N))):
        s, sn = s_ref[rows, f, :], s_ref[rows, g, :]
        p, pn = pb[pl.ds(1, N), f - YO + 4, :], hy[e]
        delta = outward(s, sn, p, pn)
        ay[e] = delta
        by[e] = outward(sn, s, pn, p)
        cy[e] = rb[rows, f, :] - delta
    for ex in (0, 1):
        rc[ex] = rx[ex]
        for ey in (0, 1):
            at = pl.ds((N - 1) * ey, 1)
            rc[ex, at, :] = rx[ex, at, :] - ay[ey, pl.ds((N - 1) * ex, 1), :]
    start([5], XSIDES)
    start([6], CORNERS)

    arrive([0], CORNERS)
    lt[pl.ds(0, 20), :] = tags(jnp.concatenate([block(0, n) for n in range(3)], axis=0))[12:]
    lt[pl.ds(52, 20), :] = tags(jnp.concatenate([block(2, n) for n in range(3)], axis=0))[:20]
    for part in (range(0, XO - 1), range(XO + N + 1, NXF)):
        coefficients(list(part), 0, NYF)
    coefficients([XO - 1, XO + N], 0, 24)
    coefficients([XO - 1, XO + N], 48, 24)
    coefficients(own_x, 0, 16)
    coefficients(own_x, 56, 16)

    for x in range(XO - 13, XO + N + 13):
        y0, ny = columns(13, x)
        at = pl.ds(y0, ny)
        s = s_ref[x, at, :]
        diag = (k_ref[x, at, :] + (s_ref[x - 4, at, :] + s_ref[x + 4, at, :])
                + (s_ref[x, pl.ds(y0 - 4, ny), :] + s_ref[x, pl.ds(y0 + 4, ny), :]))
        k_ref[x, at, :] = jnp.where(s > 0.0, 0.8 / diag, 0.0)

    sent(list(KINDS), DIRS)
    for e, (f, g) in enumerate(((XO, XO - 1), (XO + N - 1, XO + N))):
        rb[f, own, :] = rb[f, own, :] - ax[e]
    for e, (f, g) in enumerate(((YO, YO - 1), (YO + N - 1, YO + N))):
        rb[rows, f, :] = rb[rows, f, :] - ay[e]
    arrive([2, 3, 4, 5, 6], ORDER)
    for e, g in enumerate((XO - 1, XO + N)):
        @pl.when(there(XSIDES[e]))
        def _():
            rb[g, own, :] = rb[g, own, :] - bx[e]
    for e, g in enumerate((YO - 1, YO + N)):
        @pl.when(there(YSIDES[e]))
        def _():
            rb[rows, g, :] = rb[rows, g, :] - by[e]


def relax(s_ref, w_ref, k_ref, rb, res_hbm, cor_hbm, ua, pa, ub, qb, uc, ob, local):
    out_r = pltpu.make_async_copy(rb.at[pl.ds(XO, N), pl.ds(YO, N), :], res_hbm, local.at[0])
    out_r.start()

    def vertical(weight, value):
        return weight * pltpu.roll(value, DEPTH - 1, 1) + pltpu.roll(weight * value, 1, 1)

    for x in range(XO - 13, XO + N + 13):
        y0, ny = columns(13, x)
        at = pl.ds(y0, ny)
        mean = (0.5 * rb[x, at, :]
                + 0.125 * (rb[x - 1, at, :] + rb[x + 1, at, :]
                           + rb[x, pl.ds(y0 - 1, ny), :] + rb[x, pl.ds(y0 + 1, ny), :]))
        u = k_ref[x, at, :] * mean
        ua[x, at, :] = u
        pa[x, at, :] = s_ref[x, at, :] * u

    def sweep(reach, u_in, p_in, u_out, p_out, base):
        for x in range(XO - reach, XO + N + reach):
            y0, ny = columns(reach, x)
            at = pl.ds(y0, ny)
            s = s_ref[x, at, :]
            u = u_in[x, at, :]
            un = (u_in[x - 4, at, :] + u_in[x + 4, at, :]
                  + u_in[x, pl.ds(y0 - 4, ny), :] + u_in[x, pl.ds(y0 + 4, ny), :])
            pn = (p_in[x - 4, at, :] + p_in[x + 4, at, :]
                  + p_in[x, pl.ds(y0 - 4, ny), :] + p_in[x, pl.ds(y0 + 4, ny), :])
            total = s * un + pn + vertical(w_ref[x, at, :], u)
            new = base[x, at, :] + 0.2 * u + k_ref[x, at, :] * total
            u_out[x, at, :] = new
            if p_out is not None:
                p_out[x, at, :] = s * new

    sweep(9, ua, pa, ub, qb, ua)
    sweep(5, ub, qb, uc, pa, ua)
    sweep(1, uc, pa, ub, None, ua)

    def out_c(c):
        rows = pl.ds(8 * c, 8)
        return pltpu.make_async_copy(ob.at[rows], cor_hbm.at[rows], local.at[1 + c])

    for c in range(4):
        @pl.loop(8 * c, 8 * c + 8, unroll=True)
        def _(x):
            fx = x + XO
            at = pl.ds(YO, N)
            ob[x] = (0.5 * ub[fx, at, :]
                     + 0.125 * (ub[fx - 1, at, :] + ub[fx + 1, at, :]
                                + ub[fx, pl.ds(YO - 1, N), :] + ub[fx, pl.ds(YO + 1, N), :]))

        out_c(c).start()
    out_r.wait()
    for c in range(4):
        out_c(c).wait()


def per_device(pressure, source, labels, region_table):
    hbm = pl.BlockSpec(memory_space=pltpu.HBM)
    vmem = pl.BlockSpec(memory_space=pltpu.VMEM)
    own = jax.ShapeDtypeStruct((N, N, DEPTH), jnp.float32)
    field = pltpu.VMEM((NXF, NYF, DEPTH), jnp.float32)
    fields = pl.pallas_call(
        exchange,
        out_shape=(field,) * 4,
        in_specs=[hbm] * 4,
        out_specs=(vmem,) * 4,
        scratch_shapes=[
            pltpu.VMEM((N + 2, 40, DEPTH), jnp.float32),
            pltpu.VMEM((N, N, DEPTH), jnp.float32),
            pltpu.VMEM((16, DEPTH), jnp.float32),
            pltpu.VMEM((N, N), jnp.int32),
            pltpu.VMEM((8, DEPTH), jnp.int32),
            pltpu.VMEM((3, 3, 8, DEPTH), jnp.int32),
            pltpu.VMEM((NYF, DEPTH), jnp.int32),
        ] + [pltpu.VMEM((2, N, DEPTH), jnp.float32)] * 8 + [
            pltpu.VMEM((2, N, DEPTH), jnp.float32),
            pltpu.SemaphoreType.DMA((len(KEYS),)),
            pltpu.SemaphoreType.DMA((len(KEYS),)),
            pltpu.SemaphoreType.DMA((6,)),
        ],
        compiler_params=pltpu.CompilerParams(
            collective_id=0, has_side_effects=True, vmem_limit_bytes=24 << 20),
        name="exchange",
    )(*[pltpu.with_memory_space_constraint(a, pltpu.HBM)
        for a in (pressure, source, labels, region_table)])
    return pl.pallas_call(
        relax,
        out_shape=(own, own),
        in_specs=[vmem] * 4,
        out_specs=(hbm, hbm),
        scratch_shapes=[field] * 5 + [
            pltpu.VMEM((N, N, DEPTH), jnp.float32),
            pltpu.SemaphoreType.DMA((5,)),
        ],
        compiler_params=pltpu.CompilerParams(vmem_limit_bytes=24 << 20),
        name="relax",
    )(*fields)


def solution(mesh):
    placed = (P("space", "group", None), P("space", "group", None), P("space", "group"), P())
    return jax.shard_map(
        per_device,
        mesh=mesh,
        in_specs=placed,
        out_specs=(P("space", "group", None), P("space", "group", None)),
        check_vma=False,
    )
```

```python
import jax
import jax.numpy as jnp
from jax import lax
from jax.experimental import pallas as pl
from jax.experimental.pallas import tpu as pltpu
from jax.sharding import PartitionSpec as P

MESH = pl.DeviceIdType.MESH
N = 32
DEPTH = 128
XO, YO = 17, 20
NXF, NYF = 66, 72
DIRS = [(dx, dy) for dx in (-1, 0, 1) for dy in (-1, 0, 1) if (dx, dy) != (0, 0)]
ORDER = [(0, -1), (0, 1), (-1, 0), (1, 0), (-1, -1), (-1, 1), (1, -1), (1, 1)]
DIRS_X, DIRS_Y = [(-1, 0), (1, 0)], [(0, -1), (0, 1)]
DIRS_XY = [(-1, -1), (-1, 1), (1, -1), (1, 1)]
SIDES = DIRS_X + DIRS_Y


def pieces(d, stage):
    dx, dy = d
    if dy == 0:
        return [((1, 14), (1, N - 2))] if stage == (dx > 0) else []
    if dx == 0:
        return [((1, 15), (1, 14)) if stage == 0 else ((16, N - 2), (1, 14))]
    return [((2, 2), (2, 12)), ((3, 6), (2, 10)), ((7, 12), (2, 6))] if stage == (dx > 0) else []


def span(step, lo, hi):
    if step == 1:
        return N - hi, hi - lo + 1
    if step == -1:
        return lo - 1, hi - lo + 1
    return lo, hi - lo + 1


XSIDES, YSIDES, CORNERS = DIRS_X, DIRS_Y, DIRS_XY
KINDS = {0: DIRS, 1: SIDES, 2: DIRS, 3: DIRS, 4: YSIDES, 5: XSIDES, 6: CORNERS}
KEYS = [(kind, d, n) for kind, dirs in KINDS.items() for d in dirs
        for n in range(len(pieces(d, kind - 2)) if kind in (2, 3) else (1, 1, 0, 0, 2, 2, 2)[kind])]


def columns(reach, x):
    beyond = max(XO - x, x - (XO + N - 1), 1)
    side = reach - 4 * (-(-(beyond - 1) // 4))
    return YO - side - 3, -(-(N + 2 * side) // 8) * 8


def exchange(p_hbm, src_hbm, lab_hbm, tab_hbm, s_ref, w_ref, k_ref, rb,
             pb, sb, tb, lbl, pk, lpk, lt, hx, hy, ax, ay, bx, by, rx, cy, rc,
             send, recv, local):
    groups = lax.axis_size("group")
    spaces = lax.axis_size("space")
    gi = lax.axis_index("group")
    si = lax.axis_index("space")

    def there(d):
        dx, dy = d
        ok = None
        if dx == 1:
            ok = si < spaces - 1
        elif dx == -1:
            ok = si > 0
        if dy:
            okg = gi < groups - 1 if dy == 1 else gi > 0
            ok = okg if ok is None else jnp.logical_and(ok, okg)
        return ok

    def back(d):
        return (-d[0], -d[1])

    def device(d):
        return (gi + d[1], si + d[0])

    halves = ((0, 17), (17, 15))
    load_p = [pltpu.make_async_copy(p_hbm.at[pl.ds(a, n)], pb.at[pl.ds(1 + a, n), pl.ds(4, N), :],
                                    local.at[4 + h]) for h, (a, n) in enumerate(halves)]
    load_s = [pltpu.make_async_copy(src_hbm.at[pl.ds(a, n)], sb.at[pl.ds(a, n)],
                                    local.at[h]) for h, (a, n) in enumerate(halves)]
    load_l = pltpu.make_async_copy(lab_hbm, lbl, local.at[2])
    load_t = pltpu.make_async_copy(tab_hbm, tb, local.at[3])
    load_l.start()
    load_t.start()
    for h in (0, 1):
        load_p[h].start()
        load_s[h].start()

    barrier = pltpu.get_barrier_semaphore()
    count = jnp.int32(0)
    for d in DIRS:
        ok = there(d)
        count = count + ok.astype(jnp.int32)

        @pl.when(ok)
        def _():
            pl.semaphore_signal(barrier, 1, device_id=device(d), device_id_type=MESH)

    for d in DIRS:
        @pl.when(jnp.logical_not(there(d)))
        def _():
            dx, dy = d
            lpk[1 + dy, 1 + dx] = jnp.full((8, DEPTH), -1, jnp.int32)

    for d in SIDES:
        @pl.when(jnp.logical_not(there(d)))
        def _():
            dx, dy = d
            if dx:
                hx[int(dx > 0)] = jnp.zeros((N, DEPTH), jnp.float32)
                r0 = XO - 14 if dx < 0 else XO + N

                @pl.loop(0, 14)
                def _(i):
                    rb[r0 + i] = jnp.zeros((NYF, DEPTH), jnp.float32)
            else:
                hy[int(dy > 0)] = jnp.zeros((N, DEPTH), jnp.float32)
                c0 = YO - 14 if dy < 0 else YO + N

                @pl.loop(XO - 14, XO + N + 14)
                def _(i):
                    rb[i, pl.ds(c0, 14), :] = jnp.zeros((14, DEPTH), jnp.float32)

    def messages(kind, d):
        dx, dy = d
        ex, ey = int(dx > 0), int(dy > 0)
        last = N - 1
        if kind == 0:
            ends = [(pk, lpk.at[1 - dy, 1 - dx])]
        elif kind == 1:
            ends = [(p_hbm.at[last * ex], hx.at[1 - ex]) if dx
                    else (p_hbm.at[:, last * ey, :], hy.at[1 - ey])]
        elif kind in (2, 3):
            ends = []
            for rows, cols in pieces(d, kind - 2):
                x, nx = span(dx, *rows)
                y, ny = span(dy, *cols)
                x = x + XO
                y = y + YO
                ends.append((rb.at[pl.ds(x, nx), pl.ds(y, ny), :],
                             rb.at[pl.ds(x - N * dx, nx), pl.ds(y - N * dy, ny), :]))
        elif kind == 4:
            y = (N - 14) * ey
            ends = [(rx.at[e, pl.ds(y, 14), :],
                     rb.at[XO + last * e, pl.ds(YO + y - N * dy, 14), :]) for e in (0, 1)]
        elif kind == 5:
            x = (N - 14) * ex
            ends = [(cy.at[e, pl.ds(x, 14), :],
                     rb.at[pl.ds(XO + x - N * dx, 14), YO + last * e, :]) for e in (0, 1)]
        else:
            x, y = (N - 13 if ex else 1), (N - 13) * ey
            fx, fy = XO + last * ex - N * dx, YO + last * ey - N * dy
            ends = [(rc.at[ex, pl.ds(y, 13), :], rb.at[fx, pl.ds(YO + y - N * dy, 13), :]),
                    (cy.at[ey, pl.ds(x, 12), :], rb.at[pl.ds(XO + x - N * dx, 12), fy, :])]
        return [pltpu.make_async_remote_copy(
            src_ref=src, dst_ref=dst, send_sem=send.at[KEYS.index((kind, d, n))],
            recv_sem=recv.at[KEYS.index((kind, d, n))], device_id=device(d), device_id_type=MESH)
            for n, (src, dst) in enumerate(ends)]

    def held(kinds, d):
        return [k for k in kinds if any(key[:2] == (k, d) for key in KEYS)]

    def start(kinds, dirs):
        for d in dirs:
            if not held(kinds, d):
                continue

            @pl.when(there(d))
            def _():
                for kind in held(kinds, d):
                    for m in messages(kind, d):
                        m.start()

    def arrive(kinds, dirs):
        for d in dirs:
            @pl.when(there(back(d)))
            def _():
                for kind in held(kinds, d):
                    for m in messages(kind, d):
                        m.wait_recv()

    def sent(kinds, dirs):
        for d in dirs:
            @pl.when(there(d))
            def _():
                for kind in held(kinds, d):
                    for m in messages(kind, d):
                        m.wait_send()


    load_t.wait()
    half = 0.5 * tb[...]
    lane = lax.broadcasted_iota(jnp.int32, (16, DEPTH), 1)
    up = jnp.where(lane < DEPTH - 1, pltpu.roll(half, DEPTH - 1, 1), 0.0)
    down = jnp.where(lane > 0, pltpu.roll(half, 1, 1), 0.0)
    wup = jnp.where(lane < DEPTH - 1, half + up, 0.0)
    vert = 6.0 * half + (up + down)
    wide = jnp.concatenate([half, wup, vert], axis=1)
    hi = wide.astype(jnp.bfloat16)
    rest = wide - hi.astype(jnp.float32)
    mid = rest.astype(jnp.bfloat16)
    low = (rest - mid.astype(jnp.float32)).astype(jnp.bfloat16)
    table = jnp.concatenate(
        [hi, mid, low, jnp.zeros((DEPTH - 48, 3 * DEPTH), jnp.bfloat16)], axis=0)

    def tags(block):
        pad = jnp.full((N, DEPTH - 3 * N), -1, jnp.int32)
        return jnp.concatenate([block.T, pad], axis=1)

    def coefficients(xs, y0, ny):
        lanes = lax.broadcasted_iota(jnp.int32, (ny, DEPTH), 1)
        slot = jnp.where(lanes < 48, lanes & 15, -9)
        at = pl.ds(y0, ny)
        tag = lt[at, :]
        hits = []
        for x in xs:
            c = x + N - XO
            hit = jnp.broadcast_to(tag[:, c:c + 1], (ny, DEPTH)) == slot
            hits.append(jnp.where(hit, 1.0, 0.0))
        onehot = jnp.concatenate(hits, axis=0).astype(jnp.bfloat16)
        out = jnp.dot(onehot, table, preferred_element_type=jnp.float32)
        for n, x in enumerate(xs):
            part = out[n * ny:(n + 1) * ny]
            s_ref[x, at, :] = part[:, :DEPTH]
            w_ref[x, at, :] = part[:, DEPTH:2 * DEPTH]
            k_ref[x, at, :] = part[:, 2 * DEPTH:]

    own_x = list(range(XO, XO + N))
    load_l.wait()
    none = jnp.full((N, N), -1, jnp.int32)
    mine = lbl[...]
    pk[...] = jnp.concatenate([mine[8 * g:8 * g + 8] for g in range(4)], axis=1)

    def block(dy, dx):
        tile = lpk[dy, dx]
        return jnp.concatenate([tile[:, N * g:N * g + N] for g in range(4)], axis=0)

    lt[...] = jnp.full((NYF, DEPTH), -1, jnp.int32)
    lt[pl.ds(20, N), :] = tags(jnp.concatenate([none, mine, none], axis=0))

    def vertical(weight, value):
        return weight * pltpu.roll(value, DEPTH - 1, 1) + pltpu.roll(weight * value, 1, 1)

    zero = jnp.zeros((N, DEPTH), jnp.float32)
    pb[0, pl.ds(4, N), :] = zero
    pb[N + 1, pl.ds(4, N), :] = zero
    s_ref[XO - 1, pl.ds(YO, N), :] = zero
    s_ref[XO + N, pl.ds(YO, N), :] = zero
    own = pl.ds(YO, N)
    for h, (a, n) in enumerate(halves):
        coefficients(own_x[a:a + n], 16, 40)
        load_p[h].wait()
        load_s[h].wait()
        pb[pl.ds(1 + a, n), 3, :] = zero[:n]
        pb[pl.ds(1 + a, n), 4 + N, :] = zero[:n]

        @pl.loop(2 * h, 2 * h + 2)
        def _(i):
            out = []
            for x in [8 * i + n for n in range(8)]:
                fx = x + XO
                s = s_ref[fx, own, :]
                sn = [s_ref[fx - 1, own, :], s_ref[fx + 1, own, :],
                      s_ref[fx, pl.ds(YO - 1, N), :], s_ref[fx, pl.ds(YO + 1, N), :]]
                p = pb[x + 1, pl.ds(4, N), :]
                pn = [pb[x, pl.ds(4, N), :], pb[x + 2, pl.ds(4, N), :],
                      pb[x + 1, pl.ds(3, N), :], pb[x + 1, pl.ds(5, N), :]]
                flow = (s + sn[0]) * (p - pn[0])
                for n in range(1, 4):
                    flow = flow + (s + sn[n]) * (p - pn[n])
                both = k_ref[fx, own, :] - 4.0 * s
                flow = flow + (both * p - vertical(w_ref[fx, own, :], p))
                out.append(sb[x] - flow)
            for n in range(8):
                rb[8 * i + n + XO, own, :] = out[n]

        if h == 0:
            pl.semaphore_wait(barrier, count)
            start([0], ORDER)
            start([1], SIDES)
        start([2 + h], ORDER)

    def outward(s, sn, p, pn):
        return (s + sn) * (p - pn) - s * p

    arrive([0, 1], XSIDES)
    lt[pl.ds(20, N), :] = tags(jnp.concatenate([block(1, 0), mine, block(1, 2)], axis=0))
    coefficients([XO - 1, XO + N], 16, 40)
    for e, (f, g) in enumerate(((XO, XO - 1), (XO + N - 1, XO + N))):
        s, sn = s_ref[f, own, :], s_ref[g, own, :]
        p, pn = pb[f - XO + 1, pl.ds(4, N), :], hx[e]
        delta = outward(s, sn, p, pn)
        ax[e] = delta
        bx[e] = outward(sn, s, pn, p)
        rx[e] = rb[f, own, :] - delta
    start([4], YSIDES)

    arrive([0, 1], YSIDES)
    lt[pl.ds(0, 20), :] = tags(jnp.concatenate([none, block(0, 1), none], axis=0))[12:]
    lt[pl.ds(52, 20), :] = tags(jnp.concatenate([none, block(2, 1), none], axis=0))[:20]
    coefficients(own_x, 16, 8)
    coefficients(own_x, 48, 8)
    rows = pl.ds(XO, N)
    for e, (f, g) in enumerate(((YO, YO - 1), (YO + N - 1, YO + N))):
        s, sn = s_ref[rows, f, :], s_ref[rows, g, :]
        p, pn = pb[pl.ds(1, N), f - YO + 4, :], hy[e]
        delta = outward(s, sn, p, pn)
        ay[e] = delta
        by[e] = outward(sn, s, pn, p)
        cy[e] = rb[rows, f, :] - delta
    for ex in (0, 1):
        rc[ex] = rx[ex]
        for ey in (0, 1):
            at = pl.ds((N - 1) * ey, 1)
            rc[ex, at, :] = rx[ex, at, :] - ay[ey, pl.ds((N - 1) * ex, 1), :]
    start([5], XSIDES)
    start([6], CORNERS)

    arrive([0], CORNERS)
    lt[pl.ds(0, 20), :] = tags(jnp.concatenate([block(0, n) for n in range(3)], axis=0))[12:]
    lt[pl.ds(52, 20), :] = tags(jnp.concatenate([block(2, n) for n in range(3)], axis=0))[:20]
    for part in (range(0, XO - 1), range(XO + N + 1, NXF)):
        coefficients(list(part), 0, NYF)
    coefficients([XO - 1, XO + N], 0, 24)
    coefficients([XO - 1, XO + N], 48, 24)
    coefficients(own_x, 0, 16)
    coefficients(own_x, 56, 16)

    for x in range(XO - 13, XO + N + 13):
        y0, ny = columns(13, x)
        at = pl.ds(y0, ny)
        s = s_ref[x, at, :]
        diag = (k_ref[x, at, :] + (s_ref[x - 4, at, :] + s_ref[x + 4, at, :])
                + (s_ref[x, pl.ds(y0 - 4, ny), :] + s_ref[x, pl.ds(y0 + 4, ny), :]))
        k_ref[x, at, :] = jnp.where(s > 0.0, 0.8 / diag, 0.0)

    sent(list(KINDS), DIRS)
    for e, (f, g) in enumerate(((XO, XO - 1), (XO + N - 1, XO + N))):
        rb[f, own, :] = rb[f, own, :] - ax[e]
    for e, (f, g) in enumerate(((YO, YO - 1), (YO + N - 1, YO + N))):
        rb[rows, f, :] = rb[rows, f, :] - ay[e]
    arrive([2, 3, 4, 5, 6], ORDER)
    for e, g in enumerate((XO - 1, XO + N)):
        @pl.when(there(XSIDES[e]))
        def _():
            rb[g, own, :] = rb[g, own, :] - bx[e]
    for e, g in enumerate((YO - 1, YO + N)):
        @pl.when(there(YSIDES[e]))
        def _():
            rb[rows, g, :] = rb[rows, g, :] - by[e]


def relax(s_ref, w_ref, k_ref, rb, res_hbm, cor_hbm, ua, pa, ub, qb, uc, ob, local):
    out_r = pltpu.make_async_copy(rb.at[pl.ds(XO, N), pl.ds(YO, N), :], res_hbm, local.at[0])
    out_r.start()

    def vertical(weight, value):
        return weight * pltpu.roll(value, DEPTH - 1, 1) + pltpu.roll(weight * value, 1, 1)

    for x in range(XO - 13, XO + N + 13):
        y0, ny = columns(13, x)
        at = pl.ds(y0, ny)
        mean = (0.5 * rb[x, at, :]
                + 0.125 * (rb[x - 1, at, :] + rb[x + 1, at, :]
                           + rb[x, pl.ds(y0 - 1, ny), :] + rb[x, pl.ds(y0 + 1, ny), :]))
        u = k_ref[x, at, :] * mean
        ua[x, at, :] = u
        pa[x, at, :] = s_ref[x, at, :] * u

    def sweep(reach, u_in, p_in, u_out, p_out, base):
        for x in range(XO - reach, XO + N + reach):
            y0, ny = columns(reach, x)
            at = pl.ds(y0, ny)
            s = s_ref[x, at, :]
            u = u_in[x, at, :]
            un = (u_in[x - 4, at, :] + u_in[x + 4, at, :]
                  + u_in[x, pl.ds(y0 - 4, ny), :] + u_in[x, pl.ds(y0 + 4, ny), :])
            pn = (p_in[x - 4, at, :] + p_in[x + 4, at, :]
                  + p_in[x, pl.ds(y0 - 4, ny), :] + p_in[x, pl.ds(y0 + 4, ny), :])
            total = s * un + pn + vertical(w_ref[x, at, :], u)
            new = base[x, at, :] + 0.2 * u + k_ref[x, at, :] * total
            u_out[x, at, :] = new
            if p_out is not None:
                p_out[x, at, :] = s * new

    sweep(9, ua, pa, ub, qb, ua)
    sweep(5, ub, qb, uc, pa, ua)
    sweep(1, uc, pa, ub, None, ua)

    def out_c(c):
        rows = pl.ds(8 * c, 8)
        return pltpu.make_async_copy(ob.at[rows], cor_hbm.at[rows], local.at[1 + c])

    for c in range(4):
        @pl.loop(8 * c, 8 * c + 8, unroll=True)
        def _(x):
            fx = x + XO
            at = pl.ds(YO, N)
            ob[x] = (0.5 * ub[fx, at, :]
                     + 0.125 * (ub[fx - 1, at, :] + ub[fx + 1, at, :]
                                + ub[fx, pl.ds(YO - 1, N), :] + ub[fx, pl.ds(YO + 1, N), :]))

        out_c(c).start()
    out_r.wait()
    for c in range(4):
        out_c(c).wait()


def per_device(pressure, source, labels, region_table):
    hbm = pl.BlockSpec(memory_space=pltpu.HBM)
    vmem = pl.BlockSpec(memory_space=pltpu.VMEM)
    own = jax.ShapeDtypeStruct((N, N, DEPTH), jnp.float32)
    field = pltpu.VMEM((NXF, NYF, DEPTH), jnp.float32)
    fields = pl.pallas_call(
        exchange,
        out_shape=(field,) * 4,
        in_specs=[hbm] * 4,
        out_specs=(vmem,) * 4,
        scratch_shapes=[
            pltpu.VMEM((N + 2, 40, DEPTH), jnp.float32),
            pltpu.VMEM((N, N, DEPTH), jnp.float32),
            pltpu.VMEM((16, DEPTH), jnp.float32),
            pltpu.VMEM((N, N), jnp.int32),
            pltpu.VMEM((8, DEPTH), jnp.int32),
            pltpu.VMEM((3, 3, 8, DEPTH), jnp.int32),
            pltpu.VMEM((NYF, DEPTH), jnp.int32),
        ] + [pltpu.VMEM((2, N, DEPTH), jnp.float32)] * 8 + [
            pltpu.VMEM((2, N, DEPTH), jnp.float32),
            pltpu.SemaphoreType.DMA((len(KEYS),)),
            pltpu.SemaphoreType.DMA((len(KEYS),)),
            pltpu.SemaphoreType.DMA((6,)),
        ],
        compiler_params=pltpu.CompilerParams(
            collective_id=0, has_side_effects=True, vmem_limit_bytes=24 << 20),
        name="exchange",
    )(*[pltpu.with_memory_space_constraint(a, pltpu.HBM)
        for a in (pressure, source, labels, region_table)])
    return pl.pallas_call(
        relax,
        out_shape=(own, own),
        in_specs=[vmem] * 4,
        out_specs=(hbm, hbm),
        scratch_shapes=[field] * 5 + [
            pltpu.VMEM((N, N, DEPTH), jnp.float32),
            pltpu.SemaphoreType.DMA((5,)),
        ],
        compiler_params=pltpu.CompilerParams(vmem_limit_bytes=24 << 20),
        name="relax",
    )(*fields)


def solution(mesh):
    placed = (P("space", "group", None), P("space", "group", None), P("space", "group"), P())
    return jax.shard_map(
        per_device,
        mesh=mesh,
        in_specs=placed,
        out_specs=(P("space", "group", None), P("space", "group", None)),
        check_vma=False,
    )
```
